256 devices in a mesh: row: 16 (over y, x), col: 16 (over z, core).
Axes of the slice: x: 4, y: 4, z: 8, core: 2. Of those that a mesh axis runs over, the one named last changes fastest.
Arguments:
- hidden_in: bfloat16 [1024, 4096], P('col', 'row'), may hold values from -250 to 250
- norm_gain: bfloat16 [4096], P('row'), may hold values from 0.099609375 to 1.8984375
- w_qkv: bfloat16 [4096, 6144], P('row', 'col'), may hold values from -0.125 to 0.125
- w_out: bfloat16 [4096, 4096], P('row', 'col'), may hold values from -0.125 to 0.125
- cache_k: bfloat16 [16, 4096, 1024], P('col', 'row'), may hold values from -1300 to 1300
- value_cache: bfloat16 [16, 4096, 1024], P('col', 'row'), may hold values from -6 to 6
- cache_len: int32 [16], P('col'), may hold values from 1 to 4096, as said below
- parents: int32 [16, 64], P('col'), may hold values from -1 to 62, as said below
Outputs:
- update: bfloat16 [1024, 4096], P('col', 'row')
The draws below stay inside these ranges and needn't reach their ends.
Inputs may be any that keep to these rules, and one draw needn't show every extreme that they name: Slots 0 to cache_len - 1 of a request's window are filled; some request fills all 4096 slots. `parents`: slot 0 of every request is the root with parent -1; every other slot's parent is an earlier slot of the same request; slot 63 has parent 64 - 2.
All inputs are finite; a program needn't handle non-finite values.
Results may differ from the reference program's by a relative error of at most 0.011.
The reference program's roundings to bfloat16 on the way count: a program that leaves them out, or rounds other values in their place, can miss the bound.
Values may be sent and summed in bfloat16 or wider, within the bound.
A program may use at most 128 MiB of HBM per device.

```python
import jax
import jax.numpy as jnp
from jax import lax

D = 4096
QUERY_HEADS = 32
KEY_VALUE_HEADS = 8
HEAD_SIZE = 128
WINDOW_SLOTS = 4096
DRAFT_SLOTS = 64
QKV_W = 6144
REQUEST_COUNT = 16
TOKENS = 1024


def draw_hidden_in(key, part):
    key_base, k_row, k_col = jax.random.split(key, 3)
    ramp = jnp.exp(jnp.log(3.0) * jnp.arange(D, dtype=jnp.float32) / D)
    col_scale = ramp * jnp.exp(jax.random.uniform(k_col, (D,), jnp.float32, 0.0, jnp.log(10.0)))
    base_point = jnp.clip(jax.random.normal(key_base, (TOKENS, D), jnp.float32), -6.0, 6.0)
    row_scale = jnp.exp(jax.random.uniform(k_row, (TOKENS, 1), jnp.float32, 0.0, jnp.log(10.0)))
    return (base_point * row_scale * col_scale[None, :] * 0.1).astype(jnp.bfloat16)


def draw_cache_k(key, part):
    key_base = jax.random.fold_in(key, 0)
    base_point = jnp.clip(jax.random.normal(key_base, (REQUEST_COUNT, WINDOW_SLOTS, KEY_VALUE_HEADS * HEAD_SIZE), jnp.float32), -6.0, 6.0)
    return base_point.astype(jnp.bfloat16)


def draw_cache_len(key, part):
    k_len, k_full = jax.random.split(key, 2)
    lengths = jax.random.randint(k_len, (REQUEST_COUNT,), 1, WINDOW_SLOTS + 1, dtype=jnp.int32)
    fullest = jax.random.randint(k_full, (), 0, REQUEST_COUNT, dtype=jnp.int32)
    return lengths.at[fullest].set(WINDOW_SLOTS)


def draw_parents(key, part):
    uniform_bits = jax.random.randint(key, (REQUEST_COUNT, DRAFT_SLOTS), 0, 2 ** 20, dtype=jnp.int32)
    slot_ids = jnp.arange(DRAFT_SLOTS, dtype=jnp.int32)[None, :]
    chosen = uniform_bits * slot_ids // 2 ** 20
    chosen = jnp.where(slot_ids == 0, -1, chosen)
    return chosen.at[:, DRAFT_SLOTS - 1].set(DRAFT_SLOTS - 2)


def strengthened(drawn, key, source, target, parts, factor):
    owner, partner = [(jnp.arange(drawn.shape[dim]) // (drawn.shape[dim] // parts)).reshape([-1 if axis == dim else 1 for axis in range(drawn.ndim)]) for dim in (source, target)]
    chosen = jax.random.permutation(key, parts)[partner]
    strong = (owner == chosen) | (owner == (partner + parts // 2) % parts)
    return jnp.where(strong, factor * drawn, drawn)


def levels(own_key, shape, pieces, smallest, high):
    def one(dim, parts):
        draws = jax.random.uniform(jax.random.fold_in(jax.random.fold_in(own_key, 6), dim), (parts,), jnp.float32, smallest / len(pieces), high / len(pieces))
        return jnp.repeat(jnp.exp(draws), shape[dim] // parts).reshape((-1,) + (1,) * (len(shape) - dim - 1))

    factor_of = one(*pieces[0])
    for cut in pieces[1:]:
        factor_of = factor_of * one(*cut)
    return factor_of


def gaussian(stream_key, dims, width, limit, cuts=(), held_as=jnp.bfloat16):
    array = width * jax.random.normal(stream_key, dims, jnp.float32)
    if cuts:
        array = array * levels(stream_key, dims, cuts, -0.22, 0.18)
    return jnp.clip(array, -limit, limit).astype(held_as)


def heavy_noise(stream_key, shape, width, reach, cuts, heavy, kind=jnp.bfloat16):
    result = width * jax.random.normal(stream_key, shape, jnp.float32)
    if cuts:
        result = result * levels(stream_key, shape, cuts, -0.22, 0.18)
    return jnp.clip(strengthened(result, jax.random.fold_in(stream_key, 3), *heavy), -reach, reach).astype(kind)


def setup_inputs(seed: int = 0) -> dict:
    splits = jax.random.split(jax.random.key(seed), 9)
    return {
        "hidden_in": draw_hidden_in(jax.random.fold_in(splits[8], 71), 0),
        "norm_gain": jnp.clip(1.0 + 0.18 * jax.random.normal(splits[1], (D,), jnp.float32), 0.099609375, 1.8984375).astype(jnp.bfloat16),
        "w_qkv": heavy_noise(splits[2], (D, QKV_W), D ** -0.5, 0.125, ((0, 16), (1, 16)), (0, 1, 16, 2.0)),
        "w_out": heavy_noise(splits[3], (D, D), D ** -0.5, 0.125, ((0, 16), (1, 16)), (0, 1, 16, 2.0)),
        "cache_k": draw_cache_k(jax.random.fold_in(splits[8], 71), 0),
        "value_cache": gaussian(splits[5], (REQUEST_COUNT, WINDOW_SLOTS, KEY_VALUE_HEADS * HEAD_SIZE), 1.0, 6.0, ((0, 16), (1, 16))),
        "cache_len": draw_cache_len(jax.random.fold_in(splits[8], 71), 0),
        "parents": draw_parents(jax.random.fold_in(splits[8], 71), 0),
    }


masked_score = -1e+30

def ancestors(parents):
    slot_ids = jnp.arange(DRAFT_SLOTS, dtype=jnp.int32)
    parent_links = (parents[:, :, None] == slot_ids[None, None, :]).astype(jnp.float32)
    reachable = parent_links + jnp.eye(DRAFT_SLOTS, dtype=jnp.float32)[None]
    for squaring in range(max(1, (DRAFT_SLOTS - 1).bit_length())):
        product = jnp.einsum('rij,rjk->rik', reachable, reachable, precision=lax.Precision.HIGHEST)
        reachable = (product > 0.5).astype(jnp.float32)
    return reachable > 0.5

def reference(hidden_in, norm_gain, w_qkv, w_out, cache_k, value_cache, cache_len, parents):
    features = hidden_in.astype(jnp.float32)
    row_scale = lax.rsqrt(lax.optimization_barrier(jnp.mean(features * features, axis=1, keepdims=True)) + 1e-05)
    normed = (features * row_scale * norm_gain.astype(jnp.float32)[None, :]).astype(jnp.bfloat16)
    projected_output = jnp.dot(normed, w_qkv, preferred_element_type=jnp.float32).astype(jnp.bfloat16)
    head_groups = QUERY_HEADS // KEY_VALUE_HEADS
    query_block = projected_output[:, :QUERY_HEADS * HEAD_SIZE].reshape(REQUEST_COUNT, DRAFT_SLOTS, KEY_VALUE_HEADS, head_groups, HEAD_SIZE)
    new_key_block = projected_output[:, QUERY_HEADS * HEAD_SIZE:(QUERY_HEADS + KEY_VALUE_HEADS) * HEAD_SIZE].reshape(REQUEST_COUNT, DRAFT_SLOTS, KEY_VALUE_HEADS, HEAD_SIZE)
    new_value_block = projected_output[:, (QUERY_HEADS + KEY_VALUE_HEADS) * HEAD_SIZE:].reshape(REQUEST_COUNT, DRAFT_SLOTS, KEY_VALUE_HEADS, HEAD_SIZE)
    allowed = ancestors(parents)
    slot_ids = jnp.arange(WINDOW_SLOTS, dtype=jnp.int32)

    def attend(request_item):
        query_rows, fresh_key_rows, fresh_value_rows, cached_key_rows, cached_value_rows, length, tree_mask = request_item
        key_row_block = jnp.concatenate([cached_key_rows.reshape(WINDOW_SLOTS, KEY_VALUE_HEADS, HEAD_SIZE), fresh_key_rows], axis=0).astype(jnp.float32)
        value_row_block = jnp.concatenate([cached_value_rows.reshape(WINDOW_SLOTS, KEY_VALUE_HEADS, HEAD_SIZE), fresh_value_rows], axis=0).astype(jnp.float32)
        scores = jnp.einsum('tkgd,pkd->kgtp', query_rows.astype(jnp.float32), key_row_block) * HEAD_SIZE ** (-0.5)
        filled = jnp.broadcast_to((slot_ids < length)[None, :], (DRAFT_SLOTS, WINDOW_SLOTS))
        visible = jnp.concatenate([filled, tree_mask], axis=1)
        scores = jnp.where(visible, scores, masked_score)
        highest = lax.optimization_barrier(jnp.max(scores, axis=-1, keepdims=True))
        weights = jnp.where(visible, jnp.exp(scores - highest), 0.0)
        totals = lax.optimization_barrier(jnp.sum(weights, axis=-1))
        rounded = lax.optimization_barrier(weights.astype(jnp.bfloat16)).astype(jnp.float32)
        blended = jnp.einsum('kgtp,pkd->kgtd', rounded, value_row_block) / totals[..., None]
        return blended.transpose(2, 0, 1, 3).reshape(DRAFT_SLOTS, QUERY_HEADS * HEAD_SIZE).astype(jnp.bfloat16)
    attended = lax.map(attend, (query_block, new_key_block, new_value_block, cache_k, value_cache, cache_len, allowed))
    attended = attended.reshape(TOKENS, QUERY_HEADS * HEAD_SIZE)
    return jnp.dot(attended, w_out, preferred_element_type=jnp.float32).astype(jnp.bfloat16)
```

```python
import jax
import jax.numpy as jnp
from jax import lax
from jax.sharding import PartitionSpec as P

D = 4096
QUERY_HEADS = 32
KEY_VALUE_HEADS = 8
HEAD_SIZE = 128


masked_score = -1e30


def ancestors(parents):
    draft_tree = parents.shape[1]
    slot_ids = jnp.arange(draft_tree, dtype=jnp.int32)
    parent_links = (parents[:, :, None] == slot_ids[None, None, :]).astype(jnp.float32)
    reachable = parent_links + jnp.eye(draft_tree, dtype=jnp.float32)[None]
    for squaring in range(max(1, (draft_tree - 1).bit_length())):
        product = jnp.einsum("rij,rjk->rik", reachable, reachable, precision=lax.Precision.HIGHEST)
        reachable = (product > 0.5).astype(jnp.float32)
    return reachable > 0.5


def row_reduce(partial, axis_name):
    count = lax.axis_size(axis_name)
    rows, cols = partial.shape
    pieces = partial.reshape(rows, count, cols // count).transpose(1, 0, 2)
    received = lax.all_to_all(pieces, axis_name, 0, 0)
    return jnp.sum(received, axis=0)


def shards(hidden_in, norm_gain, w_qkv, w_out, cache_k, value_cache, cache_len, parents):
    rows_here = hidden_in.shape[0]
    request_list = cache_k.shape[0]
    token_positions = cache_k.shape[1]
    draft_tree = parents.shape[1]
    head_groups = QUERY_HEADS // KEY_VALUE_HEADS
    row_count = lax.axis_size("row")
    heads_dev = QUERY_HEADS // row_count
    row_index = lax.axis_index("row")
    score_scale = HEAD_SIZE ** (-0.5)
    features = hidden_in.astype(jnp.float32)
    squares = lax.psum(jnp.sum(features * features, axis=1), "row")
    row_scale = lax.rsqrt(squares / D + 1e-05)
    normed = (features * row_scale[:, None] * norm_gain.astype(jnp.float32)[None, :]).astype(
        jnp.bfloat16
    )
    partial_value = jnp.dot(
        normed, lax.all_gather(w_qkv, "col", axis=1, tiled=True), preferred_element_type=jnp.float32
    )
    summed = row_reduce(partial_value, "row").astype(jnp.bfloat16)
    projected_output = lax.all_gather(summed, "row", axis=1, tiled=True)
    query_block = projected_output[:, : QUERY_HEADS * HEAD_SIZE].reshape(
        request_list, draft_tree, KEY_VALUE_HEADS, head_groups, HEAD_SIZE
    )
    new_key_block = projected_output[
        :, QUERY_HEADS * HEAD_SIZE : (QUERY_HEADS + KEY_VALUE_HEADS) * HEAD_SIZE
    ].reshape(request_list, draft_tree, KEY_VALUE_HEADS, HEAD_SIZE)
    new_value_block = projected_output[:, (QUERY_HEADS + KEY_VALUE_HEADS) * HEAD_SIZE :].reshape(
        request_list, draft_tree, KEY_VALUE_HEADS, HEAD_SIZE
    )
    first_slot = row_index * token_positions
    slot_ids = first_slot + jnp.arange(token_positions, dtype=jnp.int32)

    def cache_part(request_item):
        query_rows, cached_key_rows, cached_value_rows, length = request_item
        key_row_block = cached_key_rows.reshape(token_positions, KEY_VALUE_HEADS, HEAD_SIZE)
        value_row_block = cached_value_rows.reshape(token_positions, KEY_VALUE_HEADS, HEAD_SIZE)
        scores = (
            jnp.einsum(
                "tkgd,pkd->kgtp", query_rows, key_row_block, preferred_element_type=jnp.float32
            )
            * score_scale
        )
        visible = (slot_ids < length)[None, None, None, :]
        scores = jnp.where(visible, scores, masked_score)
        highest = jnp.max(scores, axis=-1)
        weights = jnp.where(visible, jnp.exp(scores - highest[..., None]), 0.0)
        totals = jnp.sum(weights, axis=-1)
        blended = jnp.einsum(
            "kgtp,pkd->kgtd",
            weights.astype(jnp.bfloat16),
            value_row_block,
            preferred_element_type=jnp.float32,
        )
        stats = jnp.concatenate(
            [highest.reshape(QUERY_HEADS, draft_tree), totals.reshape(QUERY_HEADS, draft_tree)],
            axis=-1,
        )
        return jnp.concatenate(
            [blended.reshape(QUERY_HEADS, draft_tree, HEAD_SIZE), stats[:, None, :]], axis=1
        )

    packed = lax.map(cache_part, (query_block, cache_k, value_cache, cache_len))
    packed = packed.reshape(request_list, row_count, heads_dev, draft_tree + 1, HEAD_SIZE)
    gathered = lax.all_to_all(packed, "row", 1, 1)
    block_blend = gathered[:, :, :, :draft_tree, :]
    block_max = gathered[:, :, :, draft_tree, :draft_tree]
    block_total = gathered[:, :, :, draft_tree, draft_tree : 2 * draft_tree]
    allowed = ancestors(parents)[:, None, :, :]
    query_heads = projected_output[:, : QUERY_HEADS * HEAD_SIZE].reshape(
        request_list, draft_tree, QUERY_HEADS, HEAD_SIZE
    )
    query_own = lax.dynamic_slice_in_dim(query_heads, row_index * heads_dev, heads_dev, 2)
    key_own = lax.dynamic_slice_in_dim(
        jnp.repeat(new_key_block, head_groups, axis=2), row_index * heads_dev, heads_dev, 2
    )
    value_own = lax.dynamic_slice_in_dim(
        jnp.repeat(new_value_block, head_groups, axis=2), row_index * heads_dev, heads_dev, 2
    )
    tree_scores = (
        jnp.einsum("rthd,rshd->rhts", query_own, key_own, preferred_element_type=jnp.float32)
        * score_scale
    )
    tree_scores = jnp.where(allowed, tree_scores, masked_score)
    tree_max = jnp.max(tree_scores, axis=-1)
    tree_weights = jnp.where(allowed, jnp.exp(tree_scores - tree_max[..., None]), 0.0)
    tree_total = jnp.sum(tree_weights, axis=-1)
    tree_blend = jnp.einsum(
        "rhts,rshd->rhtd",
        tree_weights.astype(jnp.bfloat16),
        value_own,
        preferred_element_type=jnp.float32,
    )
    joint_max = jnp.maximum(jnp.max(block_max, axis=1), tree_max)
    block_scale = jnp.exp(block_max - joint_max[:, None])
    tree_scale = jnp.exp(tree_max - joint_max)
    numerator = jnp.sum(block_blend * block_scale[..., None], axis=1) + tree_blend * tree_scale[..., None]
    denominator = jnp.sum(block_total * block_scale, axis=1) + tree_total * tree_scale
    attended = (numerator / denominator[..., None]).astype(jnp.bfloat16)
    attended = attended.transpose(0, 2, 1, 3).reshape(rows_here, heads_dev * HEAD_SIZE)
    partial_out = jnp.dot(
        attended,
        lax.all_gather(w_out, "col", axis=1, tiled=True),
        preferred_element_type=jnp.float32,
    )
    return row_reduce(partial_out, "row").astype(jnp.bfloat16)


def solution(mesh):
    placed = (
        P("col", "row"),
        P("row"),
        P("row", "col"),
        P("row", "col"),
        P("col", "row", None),
        P("col", "row", None),
        P("col"),
        P("col", None),
    )
    return jax.shard_map(
        shards, mesh=mesh, in_specs=placed, out_specs=P("col", "row"), check_vma=False
    )
```

```python
import jax
import jax.numpy as jnp
from jax import lax
from jax.sharding import PartitionSpec as P

D = 4096
QUERY_HEADS = 32
KEY_VALUE_HEADS = 8
HEAD_SIZE = 128


masked_score = -1e30


def ancestors(parents):
    draft_tree = parents.shape[1]
    slot_ids = jnp.arange(draft_tree, dtype=jnp.int32)
    parent_links = (parents[:, :, None] == slot_ids[None, None, :]).astype(jnp.float32)
    reachable = parent_links + jnp.eye(draft_tree, dtype=jnp.float32)[None]
    for squaring in range(max(1, (draft_tree - 1).bit_length())):
        product = jnp.einsum("rij,rjk->rik", reachable, reachable, precision=lax.Precision.HIGHEST)
        reachable = (product > 0.5).astype(jnp.float32)
    return reachable > 0.5


def row_reduce(partial, axis_name, sent=jnp.float32):
    count = lax.axis_size(axis_name)
    rows, cols = partial.shape
    pieces = partial.reshape(rows, count, cols // count).transpose(1, 0, 2).astype(sent)
    received = lax.all_to_all(pieces, axis_name, 0, 0)
    return jnp.sum(received.astype(jnp.float32), axis=0)


def shards(hidden_in, norm_gain, w_qkv, w_out, cache_k, value_cache, cache_len, parents):
    rows_here = hidden_in.shape[0]
    request_list = cache_k.shape[0]
    token_positions = cache_k.shape[1]
    draft_tree = parents.shape[1]
    head_groups = QUERY_HEADS // KEY_VALUE_HEADS
    row_count = lax.axis_size("row")
    heads_dev = QUERY_HEADS // row_count
    row_index = lax.axis_index("row")
    score_scale = HEAD_SIZE ** (-0.5)
    features = hidden_in.astype(jnp.float32)
    squares = lax.psum(jnp.sum(features * features, axis=1), "row")
    row_scale = lax.rsqrt(squares / D + 1e-05)
    normed = (features * row_scale[:, None] * norm_gain.astype(jnp.float32)[None, :]).astype(
        jnp.bfloat16
    )
    partial_value = jnp.dot(
        normed, lax.all_gather(w_qkv, "col", axis=1, tiled=True), preferred_element_type=jnp.float32
    )
    summed = row_reduce(partial_value, "row").astype(jnp.bfloat16)
    projected_output = lax.all_gather(summed, "row", axis=1, tiled=True)
    query_block = projected_output[:, : QUERY_HEADS * HEAD_SIZE].reshape(
        request_list, draft_tree, KEY_VALUE_HEADS, head_groups, HEAD_SIZE
    )
    new_key_block = projected_output[
        :, QUERY_HEADS * HEAD_SIZE : (QUERY_HEADS + KEY_VALUE_HEADS) * HEAD_SIZE
    ].reshape(request_list, draft_tree, KEY_VALUE_HEADS, HEAD_SIZE)
    new_value_block = projected_output[:, (QUERY_HEADS + KEY_VALUE_HEADS) * HEAD_SIZE :].reshape(
        request_list, draft_tree, KEY_VALUE_HEADS, HEAD_SIZE
    )
    first_slot = row_index * token_positions
    slot_ids = first_slot + jnp.arange(token_positions, dtype=jnp.int32)

    def cache_part(request_item):
        query_rows, cached_key_rows, cached_value_rows, length = request_item
        key_row_block = cached_key_rows.reshape(token_positions, KEY_VALUE_HEADS, HEAD_SIZE)
        value_row_block = cached_value_rows.reshape(token_positions, KEY_VALUE_HEADS, HEAD_SIZE)
        scores = (
            jnp.einsum(
                "tkgd,pkd->kgtp", query_rows, key_row_block, preferred_element_type=jnp.float32
            )
            * score_scale
        )
        visible = (slot_ids < length)[None, None, None, :]
        scores = jnp.where(visible, scores, masked_score)
        highest = jnp.max(scores, axis=-1).astype(jnp.bfloat16).astype(jnp.float32)
        weights = jnp.where(visible, jnp.exp(scores - highest[..., None]), 0.0)
        totals = jnp.sum(weights, axis=-1)
        blended = jnp.einsum(
            "kgtp,pkd->kgtd",
            weights.astype(jnp.bfloat16),
            value_row_block,
            preferred_element_type=jnp.float32,
        )
        stats = jnp.concatenate(
            [highest.reshape(QUERY_HEADS, draft_tree), totals.reshape(QUERY_HEADS, draft_tree)],
            axis=-1,
        )
        return jnp.concatenate(
            [blended.reshape(QUERY_HEADS, draft_tree, HEAD_SIZE), stats[:, None, :]], axis=1
        ).astype(jnp.bfloat16)

    packed = lax.map(cache_part, (query_block, cache_k, value_cache, cache_len))
    packed = packed.reshape(request_list, row_count, heads_dev, draft_tree + 1, HEAD_SIZE)
    gathered = lax.all_to_all(packed, "row", 1, 1).astype(jnp.float32)
    block_blend = gathered[:, :, :, :draft_tree, :]
    block_max = gathered[:, :, :, draft_tree, :draft_tree]
    block_total = gathered[:, :, :, draft_tree, draft_tree : 2 * draft_tree]
    allowed = ancestors(parents)[:, None, :, :]
    query_heads = projected_output[:, : QUERY_HEADS * HEAD_SIZE].reshape(
        request_list, draft_tree, QUERY_HEADS, HEAD_SIZE
    )
    query_own = lax.dynamic_slice_in_dim(query_heads, row_index * heads_dev, heads_dev, 2)
    key_own = lax.dynamic_slice_in_dim(
        jnp.repeat(new_key_block, head_groups, axis=2), row_index * heads_dev, heads_dev, 2
    )
    value_own = lax.dynamic_slice_in_dim(
        jnp.repeat(new_value_block, head_groups, axis=2), row_index * heads_dev, heads_dev, 2
    )
    tree_scores = (
        jnp.einsum("rthd,rshd->rhts", query_own, key_own, preferred_element_type=jnp.float32)
        * score_scale
    )
    tree_scores = jnp.where(allowed, tree_scores, masked_score)
    tree_max = jnp.max(tree_scores, axis=-1)
    tree_weights = jnp.where(allowed, jnp.exp(tree_scores - tree_max[..., None]), 0.0)
    tree_total = jnp.sum(tree_weights, axis=-1)
    tree_blend = jnp.einsum(
        "rhts,rshd->rhtd",
        tree_weights.astype(jnp.bfloat16),
        value_own,
        preferred_element_type=jnp.float32,
    )
    joint_max = jnp.maximum(jnp.max(block_max, axis=1), tree_max)
    block_scale = jnp.exp(block_max - joint_max[:, None])
    tree_scale = jnp.exp(tree_max - joint_max)
    numerator = jnp.sum(block_blend * block_scale[..., None], axis=1) + tree_blend * tree_scale[..., None]
    denominator = jnp.sum(block_total * block_scale, axis=1) + tree_total * tree_scale
    attended = (numerator / denominator[..., None]).astype(jnp.bfloat16)
    attended = attended.transpose(0, 2, 1, 3).reshape(rows_here, heads_dev * HEAD_SIZE)
    partial_out = jnp.dot(
        attended,
        lax.all_gather(w_out, "col", axis=1, tiled=True),
        preferred_element_type=jnp.float32,
    )
    return row_reduce(partial_out, "row", jnp.bfloat16).astype(jnp.bfloat16)


def solution(mesh):
    placed = (
        P("col", "row"),
        P("row"),
        P("row", "col"),
        P("row", "col"),
        P("col", "row", None),
        P("col", "row", None),
        P("col"),
        P("col", None),
    )
    return jax.shard_map(
        shards, mesh=mesh, in_specs=placed, out_specs=P("col", "row"), check_vma=False
    )
```

```python
import jax
import jax.numpy as jnp
from jax import lax
from jax.sharding import PartitionSpec as P

D = 4096
QUERY_HEADS = 32
KEY_VALUE_HEADS = 8
HEAD_SIZE = 128


masked_score = -1e30


def ancestors(parents):
    draft_tree = parents.shape[1]
    slot_ids = jnp.arange(draft_tree, dtype=jnp.int32)
    parent_links = (parents[:, :, None] == slot_ids[None, None, :]).astype(jnp.float32)
    reachable = parent_links + jnp.eye(draft_tree, dtype=jnp.float32)[None]
    for squaring in range(max(1, (draft_tree - 1).bit_length())):
        product = jnp.einsum("rij,rjk->rik", reachable, reachable, precision=lax.Precision.HIGHEST)
        reachable = (product > 0.5).astype(jnp.float32)
    return reachable > 0.5


def row_reduce(partial, axis_name, sent=jnp.float32):
    count = lax.axis_size(axis_name)
    rows, cols = partial.shape
    pieces = partial.reshape(rows, count, cols // count).transpose(1, 0, 2).astype(sent)
    received = lax.all_to_all(pieces, axis_name, 0, 0)
    return jnp.sum(received.astype(jnp.float32), axis=0)


def row_gather(value, axis_name):
    count = lax.axis_size(axis_name)
    copies = jnp.broadcast_to(value[None], (count,) + value.shape)
    return lax.all_to_all(copies, axis_name, 0, 0)


def shards(hidden_in, norm_gain, w_qkv, w_out, cache_k, value_cache, cache_len, parents):
    rows_here = hidden_in.shape[0]
    request_list = cache_k.shape[0]
    token_positions = cache_k.shape[1]
    draft_tree = parents.shape[1]
    head_groups = QUERY_HEADS // KEY_VALUE_HEADS
    row_count = lax.axis_size("row")
    heads_dev = QUERY_HEADS // row_count
    row_index = lax.axis_index("row")
    score_scale = HEAD_SIZE ** (-0.5)
    features = hidden_in.astype(jnp.float32)
    squares = jnp.sum(row_gather(jnp.sum(features * features, axis=1), "row"), axis=0)
    row_scale = lax.rsqrt(squares / D + 1e-05)
    normed = (features * row_scale[:, None] * norm_gain.astype(jnp.float32)[None, :]).astype(
        jnp.bfloat16
    )
    partial_value = jnp.dot(
        normed, lax.all_gather(w_qkv, "col", axis=1, tiled=True), preferred_element_type=jnp.float32
    )
    summed = row_reduce(partial_value, "row").astype(jnp.bfloat16)
    projected_output = row_gather(summed, "row").transpose(1, 0, 2).reshape(rows_here, -1)
    query_block = projected_output[:, : QUERY_HEADS * HEAD_SIZE].reshape(
        request_list, draft_tree, KEY_VALUE_HEADS, head_groups, HEAD_SIZE
    )
    new_key_block = projected_output[
        :, QUERY_HEADS * HEAD_SIZE : (QUERY_HEADS + KEY_VALUE_HEADS) * HEAD_SIZE
    ].reshape(request_list, draft_tree, KEY_VALUE_HEADS, HEAD_SIZE)
    new_value_block = projected_output[:, (QUERY_HEADS + KEY_VALUE_HEADS) * HEAD_SIZE :].reshape(
        request_list, draft_tree, KEY_VALUE_HEADS, HEAD_SIZE
    )
    first_slot = row_index * token_positions
    slot_ids = first_slot + jnp.arange(token_positions, dtype=jnp.int32)

    def cache_part(request_item):
        query_rows, cached_key_rows, cached_value_rows, length = request_item
        key_row_block = cached_key_rows.reshape(token_positions, KEY_VALUE_HEADS, HEAD_SIZE)
        value_row_block = cached_value_rows.reshape(token_positions, KEY_VALUE_HEADS, HEAD_SIZE)
        scores = (
            jnp.einsum(
                "tkgd,pkd->kgtp", query_rows, key_row_block, preferred_element_type=jnp.float32
            )
            * score_scale
        )
        visible = (slot_ids < length)[None, None, None, :]
        scores = jnp.where(visible, scores, masked_score)
        highest = jnp.max(scores, axis=-1).astype(jnp.bfloat16).astype(jnp.float32)
        weights = jnp.where(visible, jnp.exp(scores - highest[..., None]), 0.0)
        totals = jnp.sum(weights, axis=-1)
        blended = jnp.einsum(
            "kgtp,pkd->kgtd",
            weights.astype(jnp.bfloat16),
            value_row_block,
            preferred_element_type=jnp.float32,
        )
        stats = jnp.concatenate(
            [highest.reshape(QUERY_HEADS, draft_tree), totals.reshape(QUERY_HEADS, draft_tree)],
            axis=-1,
        )
        return jnp.concatenate(
            [blended.reshape(QUERY_HEADS, draft_tree, HEAD_SIZE), stats[:, None, :]], axis=1
        ).astype(jnp.bfloat16)

    packed = lax.map(cache_part, (query_block, cache_k, value_cache, cache_len))
    packed = packed.reshape(request_list, row_count, heads_dev, draft_tree + 1, HEAD_SIZE)
    gathered = lax.all_to_all(packed, "row", 1, 1).astype(jnp.float32)
    block_blend = gathered[:, :, :, :draft_tree, :]
    block_max = gathered[:, :, :, draft_tree, :draft_tree]
    block_total = gathered[:, :, :, draft_tree, draft_tree : 2 * draft_tree]
    allowed = ancestors(parents)[:, None, :, :]
    query_heads = projected_output[:, : QUERY_HEADS * HEAD_SIZE].reshape(
        request_list, draft_tree, QUERY_HEADS, HEAD_SIZE
    )
    query_own = lax.dynamic_slice_in_dim(query_heads, row_index * heads_dev, heads_dev, 2)
    key_own = lax.dynamic_slice_in_dim(
        jnp.repeat(new_key_block, head_groups, axis=2), row_index * heads_dev, heads_dev, 2
    )
    value_own = lax.dynamic_slice_in_dim(
        jnp.repeat(new_value_block, head_groups, axis=2), row_index * heads_dev, heads_dev, 2
    )
    tree_scores = (
        jnp.einsum("rthd,rshd->rhts", query_own, key_own, preferred_element_type=jnp.float32)
        * score_scale
    )
    tree_scores = jnp.where(allowed, tree_scores, masked_score)
    tree_max = jnp.max(tree_scores, axis=-1)
    tree_weights = jnp.where(allowed, jnp.exp(tree_scores - tree_max[..., None]), 0.0)
    tree_total = jnp.sum(tree_weights, axis=-1)
    tree_blend = jnp.einsum(
        "rhts,rshd->rhtd",
        tree_weights.astype(jnp.bfloat16),
        value_own,
        preferred_element_type=jnp.float32,
    )
    joint_max = jnp.maximum(jnp.max(block_max, axis=1), tree_max)
    block_scale = jnp.exp(block_max - joint_max[:, None])
    tree_scale = jnp.exp(tree_max - joint_max)
    numerator = jnp.sum(block_blend * block_scale[..., None], axis=1) + tree_blend * tree_scale[..., None]
    denominator = jnp.sum(block_total * block_scale, axis=1) + tree_total * tree_scale
    attended = (numerator / denominator[..., None]).astype(jnp.bfloat16)
    attended = attended.transpose(0, 2, 1, 3).reshape(rows_here, heads_dev * HEAD_SIZE)
    partial_out = jnp.dot(
        attended,
        lax.all_gather(w_out, "col", axis=1, tiled=True),
        preferred_element_type=jnp.float32,
    )
    return row_reduce(partial_out, "row", jnp.bfloat16).astype(jnp.bfloat16)


def solution(mesh):
    placed = (
        P("col", "row"),
        P("row"),
        P("row", "col"),
        P("row", "col"),
        P("col", "row", None),
        P("col", "row", None),
        P("col"),
        P("col", None),
    )
    return jax.shard_map(
        shards, mesh=mesh, in_specs=placed, out_specs=P("col", "row"), check_vma=False
    )
```

```python
import jax
import jax.numpy as jnp
from jax import lax
from jax.sharding import PartitionSpec as P

D = 4096
QUERY_HEADS = 32
KEY_VALUE_HEADS = 8
HEAD_SIZE = 128


masked_score = -1e30


def ancestors(parents):
    draft_tree = parents.shape[1]
    slot_ids = jnp.arange(draft_tree, dtype=jnp.int32)
    parent_links = (parents[:, :, None] == slot_ids[None, None, :]).astype(jnp.float32)
    reachable = parent_links + jnp.eye(draft_tree, dtype=jnp.float32)[None]
    for squaring in range(max(1, (draft_tree - 1).bit_length())):
        product = jnp.einsum("rij,rjk->rik", reachable, reachable, precision=lax.Precision.HIGHEST)
        reachable = (product > 0.5).astype(jnp.float32)
    return reachable > 0.5


def row_reduce(partial, axis_name, sent=jnp.float32):
    count = lax.axis_size(axis_name)
    rows, cols = partial.shape
    pieces = partial.reshape(rows, count, cols // count).transpose(1, 0, 2).astype(sent)
    received = lax.all_to_all(pieces, axis_name, 0, 0)
    return jnp.sum(received.astype(jnp.float32), axis=0)


def row_gather(value, axis_name):
    count = lax.axis_size(axis_name)
    copies = jnp.broadcast_to(value[None], (count,) + value.shape)
    return lax.all_to_all(copies, axis_name, 0, 0)


def shards(hidden_in, norm_gain, w_qkv, w_out, cache_k, value_cache, cache_len, parents):
    rows_here = hidden_in.shape[0]
    request_list = cache_k.shape[0]
    token_positions = cache_k.shape[1]
    draft_tree = parents.shape[1]
    head_groups = QUERY_HEADS // KEY_VALUE_HEADS
    row_count = lax.axis_size("row")
    heads_dev = QUERY_HEADS // row_count
    row_index = lax.axis_index("row")
    score_scale = HEAD_SIZE ** (-0.5)
    features = hidden_in.astype(jnp.float32)
    squares = jnp.sum(row_gather(jnp.sum(features * features, axis=1), "row"), axis=0)
    row_scale = lax.rsqrt(squares / D + 1e-05)
    normed = (features * row_scale[:, None] * norm_gain.astype(jnp.float32)[None, :]).astype(
        jnp.bfloat16
    )
    col_count = lax.axis_size("col")
    all_tokens = row_gather(normed, "col").reshape(col_count * rows_here, -1)
    partial_value = jnp.dot(all_tokens, w_qkv, preferred_element_type=jnp.float32)
    received = lax.all_to_all(
        partial_value.reshape(col_count, rows_here, -1), "row", 0, 0
    )
    summed = jnp.sum(received, axis=0).astype(jnp.bfloat16)
    transpose = [
        (r * col_count + c, c * col_count + r) for r in range(row_count) for c in range(col_count)
    ]
    summed = lax.ppermute(summed, ("row", "col"), transpose)
    projected_output = row_gather(summed, "row").transpose(1, 0, 2).reshape(rows_here, -1)
    query_block = projected_output[:, : QUERY_HEADS * HEAD_SIZE].reshape(
        request_list, draft_tree, KEY_VALUE_HEADS, head_groups, HEAD_SIZE
    )
    new_key_block = projected_output[
        :, QUERY_HEADS * HEAD_SIZE : (QUERY_HEADS + KEY_VALUE_HEADS) * HEAD_SIZE
    ].reshape(request_list, draft_tree, KEY_VALUE_HEADS, HEAD_SIZE)
    new_value_block = projected_output[:, (QUERY_HEADS + KEY_VALUE_HEADS) * HEAD_SIZE :].reshape(
        request_list, draft_tree, KEY_VALUE_HEADS, HEAD_SIZE
    )
    first_slot = row_index * token_positions
    slot_ids = first_slot + jnp.arange(token_positions, dtype=jnp.int32)

    def cache_part(request_item):
        query_rows, cached_key_rows, cached_value_rows, length = request_item
        key_row_block = cached_key_rows.reshape(token_positions, KEY_VALUE_HEADS, HEAD_SIZE)
        value_row_block = cached_value_rows.reshape(token_positions, KEY_VALUE_HEADS, HEAD_SIZE)
        scores = (
            jnp.einsum(
                "tkgd,pkd->kgtp", query_rows, key_row_block, preferred_element_type=jnp.float32
            )
            * score_scale
        )
        visible = (slot_ids < length)[None, None, None, :]
        scores = jnp.where(visible, scores, masked_score)
        highest = jnp.max(scores, axis=-1).astype(jnp.bfloat16).astype(jnp.float32)
        weights = jnp.where(visible, jnp.exp(scores - highest[..., None]), 0.0)
        totals = jnp.sum(weights, axis=-1)
        blended = jnp.einsum(
            "kgtp,pkd->kgtd",
            weights.astype(jnp.bfloat16),
            value_row_block,
            preferred_element_type=jnp.float32,
        )
        stats = jnp.concatenate(
            [highest.reshape(QUERY_HEADS, draft_tree), totals.reshape(QUERY_HEADS, draft_tree)],
            axis=-1,
        )
        return jnp.concatenate(
            [blended.reshape(QUERY_HEADS, draft_tree, HEAD_SIZE), stats[:, None, :]], axis=1
        ).astype(jnp.bfloat16)

    packed = lax.map(cache_part, (query_block, cache_k, value_cache, cache_len))
    packed = packed.reshape(request_list, row_count, heads_dev, draft_tree + 1, HEAD_SIZE)
    gathered = lax.all_to_all(packed, "row", 1, 1).astype(jnp.float32)
    block_blend = gathered[:, :, :, :draft_tree, :]
    block_max = gathered[:, :, :, draft_tree, :draft_tree]
    block_total = gathered[:, :, :, draft_tree, draft_tree : 2 * draft_tree]
    allowed = ancestors(parents)[:, None, :, :]
    query_heads = projected_output[:, : QUERY_HEADS * HEAD_SIZE].reshape(
        request_list, draft_tree, QUERY_HEADS, HEAD_SIZE
    )
    query_own = lax.dynamic_slice_in_dim(query_heads, row_index * heads_dev, heads_dev, 2)
    key_own = lax.dynamic_slice_in_dim(
        jnp.repeat(new_key_block, head_groups, axis=2), row_index * heads_dev, heads_dev, 2
    )
    value_own = lax.dynamic_slice_in_dim(
        jnp.repeat(new_value_block, head_groups, axis=2), row_index * heads_dev, heads_dev, 2
    )
    tree_scores = (
        jnp.einsum("rthd,rshd->rhts", query_own, key_own, preferred_element_type=jnp.float32)
        * score_scale
    )
    tree_scores = jnp.where(allowed, tree_scores, masked_score)
    tree_max = jnp.max(tree_scores, axis=-1)
    tree_weights = jnp.where(allowed, jnp.exp(tree_scores - tree_max[..., None]), 0.0)
    tree_total = jnp.sum(tree_weights, axis=-1)
    tree_blend = jnp.einsum(
        "rhts,rshd->rhtd",
        tree_weights.astype(jnp.bfloat16),
        value_own,
        preferred_element_type=jnp.float32,
    )
    joint_max = jnp.maximum(jnp.max(block_max, axis=1), tree_max)
    block_scale = jnp.exp(block_max - joint_max[:, None])
    tree_scale = jnp.exp(tree_max - joint_max)
    numerator = jnp.sum(block_blend * block_scale[..., None], axis=1) + tree_blend * tree_scale[..., None]
    denominator = jnp.sum(block_total * block_scale, axis=1) + tree_total * tree_scale
    attended = (numerator / denominator[..., None]).astype(jnp.bfloat16)
    attended = attended.transpose(0, 2, 1, 3).reshape(rows_here, heads_dev * HEAD_SIZE)
    partial_out = jnp.dot(
        attended,
        lax.all_gather(w_out, "col", axis=1, tiled=True),
        preferred_element_type=jnp.float32,
    )
    return row_reduce(partial_out, "row", jnp.bfloat16).astype(jnp.bfloat16)


def solution(mesh):
    placed = (
        P("col", "row"),
        P("row"),
        P("row", "col"),
        P("row", "col"),
        P("col", "row", None),
        P("col", "row", None),
        P("col"),
        P("col", None),
    )
    return jax.shard_map(
        shards, mesh=mesh, in_specs=placed, out_specs=P("col", "row"), check_vma=False
    )
```

```python
import jax
import jax.numpy as jnp
from jax import lax
from jax.sharding import PartitionSpec as P

D = 4096
QUERY_HEADS = 32
KEY_VALUE_HEADS = 8
HEAD_SIZE = 128


masked_score = -1e30


def ancestors(parents):
    draft_tree = parents.shape[1]
    slot_ids = jnp.arange(draft_tree, dtype=jnp.int32)
    parent_links = (parents[:, :, None] == slot_ids[None, None, :]).astype(jnp.float32)
    reachable = parent_links + jnp.eye(draft_tree, dtype=jnp.float32)[None]
    for squaring in range(max(1, (draft_tree - 1).bit_length())):
        product = jnp.einsum("rij,rjk->rik", reachable, reachable, precision=lax.Precision.HIGHEST)
        reachable = (product > 0.5).astype(jnp.float32)
    return reachable > 0.5


def row_reduce(partial, axis_name, sent=jnp.float32):
    count = lax.axis_size(axis_name)
    rows, cols = partial.shape
    pieces = partial.reshape(rows, count, cols // count).transpose(1, 0, 2).astype(sent)
    received = lax.all_to_all(pieces, axis_name, 0, 0)
    return jnp.sum(received.astype(jnp.float32), axis=0)


def row_gather(value, axis_name):
    count = lax.axis_size(axis_name)
    copies = jnp.broadcast_to(value[None], (count,) + value.shape)
    return lax.all_to_all(copies, axis_name, 0, 0)


def shards(hidden_in, norm_gain, w_qkv, w_out, cache_k, value_cache, cache_len, parents):
    rows_here = hidden_in.shape[0]
    request_list = cache_k.shape[0]
    token_positions = cache_k.shape[1]
    draft_tree = parents.shape[1]
    head_groups = QUERY_HEADS // KEY_VALUE_HEADS
    row_count = lax.axis_size("row")
    heads_dev = QUERY_HEADS // row_count
    row_index = lax.axis_index("row")
    score_scale = HEAD_SIZE ** (-0.5)
    features = hidden_in.astype(jnp.float32)
    squares = jnp.sum(row_gather(jnp.sum(features * features, axis=1), "row"), axis=0)
    row_scale = lax.rsqrt(squares / D + 1e-05)
    normed = (features * row_scale[:, None] * norm_gain.astype(jnp.float32)[None, :]).astype(
        jnp.bfloat16
    )
    col_count = lax.axis_size("col")
    all_tokens = lax.all_gather(normed, "col", axis=0, tiled=True)
    w_out, all_tokens = lax.optimization_barrier((w_out, all_tokens))
    partial_value = jnp.dot(all_tokens, w_qkv, preferred_element_type=jnp.float32)
    received = lax.all_to_all(
        partial_value.reshape(col_count, rows_here, -1), "row", 0, 0
    )
    summed = jnp.sum(received, axis=0).astype(jnp.bfloat16)
    transpose = [
        (r * col_count + c, c * col_count + r) for r in range(row_count) for c in range(col_count)
    ]
    summed = lax.ppermute(summed, ("row", "col"), transpose)
    projected_output = row_gather(summed, "row").transpose(1, 0, 2).reshape(rows_here, -1)
    query_block = projected_output[:, : QUERY_HEADS * HEAD_SIZE].reshape(
        request_list, draft_tree, KEY_VALUE_HEADS, head_groups, HEAD_SIZE
    )
    new_key_block = projected_output[
        :, QUERY_HEADS * HEAD_SIZE : (QUERY_HEADS + KEY_VALUE_HEADS) * HEAD_SIZE
    ].reshape(request_list, draft_tree, KEY_VALUE_HEADS, HEAD_SIZE)
    new_value_block = projected_output[:, (QUERY_HEADS + KEY_VALUE_HEADS) * HEAD_SIZE :].reshape(
        request_list, draft_tree, KEY_VALUE_HEADS, HEAD_SIZE
    )
    first_slot = row_index * token_positions
    slot_ids = first_slot + jnp.arange(token_positions, dtype=jnp.int32)

    def cache_part(request_item):
        query_rows, cached_key_rows, cached_value_rows, length = request_item
        key_row_block = cached_key_rows.reshape(token_positions, KEY_VALUE_HEADS, HEAD_SIZE)
        value_row_block = cached_value_rows.reshape(token_positions, KEY_VALUE_HEADS, HEAD_SIZE)
        scores = (
            jnp.einsum(
                "tkgd,pkd->kgtp", query_rows, key_row_block, preferred_element_type=jnp.float32
            )
            * score_scale
        )
        visible = (slot_ids < length)[None, None, None, :]
        scores = jnp.where(visible, scores, masked_score)
        highest = jnp.max(scores, axis=-1).astype(jnp.bfloat16).astype(jnp.float32)
        weights = jnp.where(visible, jnp.exp(scores - highest[..., None]), 0.0)
        totals = jnp.sum(weights, axis=-1)
        blended = jnp.einsum(
            "kgtp,pkd->kgtd",
            weights.astype(jnp.bfloat16),
            value_row_block,
            preferred_element_type=jnp.float32,
        )
        stats = jnp.concatenate(
            [highest.reshape(QUERY_HEADS, draft_tree), totals.reshape(QUERY_HEADS, draft_tree)],
            axis=-1,
        )
        return jnp.concatenate(
            [blended.reshape(QUERY_HEADS, draft_tree, HEAD_SIZE), stats[:, None, :]], axis=1
        ).astype(jnp.bfloat16)

    packed = lax.map(cache_part, (query_block, cache_k, value_cache, cache_len))
    packed = packed.reshape(request_list, row_count, heads_dev, draft_tree + 1, HEAD_SIZE)
    gathered = lax.all_to_all(packed, "row", 1, 1).astype(jnp.float32)
    block_blend = gathered[:, :, :, :draft_tree, :]
    block_max = gathered[:, :, :, draft_tree, :draft_tree]
    block_total = gathered[:, :, :, draft_tree, draft_tree : 2 * draft_tree]
    allowed = ancestors(parents)[:, None, :, :]
    query_heads = projected_output[:, : QUERY_HEADS * HEAD_SIZE].reshape(
        request_list, draft_tree, QUERY_HEADS, HEAD_SIZE
    )
    query_own = lax.dynamic_slice_in_dim(query_heads, row_index * heads_dev, heads_dev, 2)
    key_own = lax.dynamic_slice_in_dim(
        jnp.repeat(new_key_block, head_groups, axis=2), row_index * heads_dev, heads_dev, 2
    )
    value_own = lax.dynamic_slice_in_dim(
        jnp.repeat(new_value_block, head_groups, axis=2), row_index * heads_dev, heads_dev, 2
    )
    tree_scores = (
        jnp.einsum("rthd,rshd->rhts", query_own, key_own, preferred_element_type=jnp.float32)
        * score_scale
    )
    tree_scores = jnp.where(allowed, tree_scores, masked_score)
    tree_max = jnp.max(tree_scores, axis=-1)
    tree_weights = jnp.where(allowed, jnp.exp(tree_scores - tree_max[..., None]), 0.0)
    tree_total = jnp.sum(tree_weights, axis=-1)
    tree_blend = jnp.einsum(
        "rhts,rshd->rhtd",
        tree_weights.astype(jnp.bfloat16),
        value_own,
        preferred_element_type=jnp.float32,
    )
    joint_max = jnp.maximum(jnp.max(block_max, axis=1), tree_max)
    block_scale = jnp.exp(block_max - joint_max[:, None])
    tree_scale = jnp.exp(tree_max - joint_max)
    numerator = jnp.sum(block_blend * block_scale[..., None], axis=1) + tree_blend * tree_scale[..., None]
    denominator = jnp.sum(block_total * block_scale, axis=1) + tree_total * tree_scale
    attended = (numerator / denominator[..., None]).astype(jnp.bfloat16)
    attended = attended.transpose(0, 2, 1, 3).reshape(rows_here, heads_dev * HEAD_SIZE)
    partial_out = jnp.dot(
        attended,
        lax.all_gather(w_out, "col", axis=1, tiled=True),
        preferred_element_type=jnp.float32,
    )
    return row_reduce(partial_out, "row", jnp.bfloat16).astype(jnp.bfloat16)


def solution(mesh):
    placed = (
        P("col", "row"),
        P("row"),
        P("row", "col"),
        P("row", "col"),
        P("col", "row", None),
        P("col", "row", None),
        P("col"),
        P("col", None),
    )
    return jax.shard_map(
        shards, mesh=mesh, in_specs=placed, out_specs=P("col", "row"), check_vma=False
    )
```

```python
import jax
import jax.numpy as jnp
from jax import lax
from jax.sharding import PartitionSpec as P

D = 4096
QUERY_HEADS = 32
KEY_VALUE_HEADS = 8
HEAD_SIZE = 128


masked_score = -1e30


def ancestors(parents):
    draft_tree = parents.shape[1]
    slot_ids = jnp.arange(draft_tree, dtype=jnp.int32)
    parent_links = (parents[:, :, None] == slot_ids[None, None, :]).astype(jnp.float32)
    reachable = parent_links + jnp.eye(draft_tree, dtype=jnp.float32)[None]
    for squaring in range(max(1, (draft_tree - 1).bit_length())):
        product = jnp.einsum("rij,rjk->rik", reachable, reachable, precision=lax.Precision.HIGHEST)
        reachable = (product > 0.5).astype(jnp.float32)
    return reachable > 0.5


def row_reduce(partial, axis_name, sent=jnp.float32):
    count = lax.axis_size(axis_name)
    rows, cols = partial.shape
    pieces = partial.reshape(rows, count, cols // count).transpose(1, 0, 2).astype(sent)
    received = lax.all_to_all(pieces, axis_name, 0, 0)
    return jnp.sum(received.astype(jnp.float32), axis=0)


def row_gather(value, axis_name):
    count = lax.axis_size(axis_name)
    copies = jnp.broadcast_to(value[None], (count,) + value.shape)
    return lax.all_to_all(copies, axis_name, 0, 0)


def shards(hidden_in, norm_gain, w_qkv, w_out, cache_k, value_cache, cache_len, parents):
    rows_here = hidden_in.shape[0]
    request_list = cache_k.shape[0]
    token_positions = cache_k.shape[1]
    draft_tree = parents.shape[1]
    head_groups = QUERY_HEADS // KEY_VALUE_HEADS
    row_count = lax.axis_size("row")
    heads_dev = QUERY_HEADS // row_count
    row_index = lax.axis_index("row")
    score_scale = HEAD_SIZE ** (-0.5)
    features = hidden_in.astype(jnp.float32)
    squares = jnp.sum(row_gather(jnp.sum(features * features, axis=1), "row"), axis=0)
    row_scale = lax.rsqrt(squares / D + 1e-05)
    normed = (features * row_scale[:, None] * norm_gain.astype(jnp.float32)[None, :]).astype(
        jnp.bfloat16
    )
    partial_value = jnp.dot(
        normed, lax.all_gather(w_qkv, "col", axis=1, tiled=True), preferred_element_type=jnp.float32
    )
    summed = row_reduce(partial_value, "row").astype(jnp.bfloat16)
    projected_output = row_gather(summed, "row").transpose(1, 0, 2).reshape(rows_here, -1)
    query_block = projected_output[:, : QUERY_HEADS * HEAD_SIZE].reshape(
        request_list, draft_tree, KEY_VALUE_HEADS, head_groups, HEAD_SIZE
    )
    new_key_block = projected_output[
        :, QUERY_HEADS * HEAD_SIZE : (QUERY_HEADS + KEY_VALUE_HEADS) * HEAD_SIZE
    ].reshape(request_list, draft_tree, KEY_VALUE_HEADS, HEAD_SIZE)
    new_value_block = projected_output[:, (QUERY_HEADS + KEY_VALUE_HEADS) * HEAD_SIZE :].reshape(
        request_list, draft_tree, KEY_VALUE_HEADS, HEAD_SIZE
    )
    first_slot = row_index * token_positions
    slot_ids = first_slot + jnp.arange(token_positions, dtype=jnp.int32)

    def cache_part(request_item):
        query_rows, cached_key_rows, cached_value_rows, length = request_item
        key_row_block = cached_key_rows.reshape(token_positions, KEY_VALUE_HEADS, HEAD_SIZE)
        value_row_block = cached_value_rows.reshape(token_positions, KEY_VALUE_HEADS, HEAD_SIZE)
        scores = (
            jnp.einsum(
                "tkgd,pkd->kgtp", query_rows, key_row_block, preferred_element_type=jnp.float32
            )
            * score_scale
        )
        visible = (slot_ids < length)[None, None, None, :]
        scores = jnp.where(visible, scores, masked_score)
        highest = jnp.max(scores, axis=-1)
        weights = jnp.where(visible, jnp.exp(scores - highest[..., None]), 0.0)
        totals = jnp.sum(weights, axis=-1)
        blended = jnp.einsum(
            "kgtp,pkd->kgtd",
            weights.astype(jnp.bfloat16),
            value_row_block,
            preferred_element_type=jnp.float32,
        )
        highest = highest.reshape(QUERY_HEADS, draft_tree)
        max_hi = highest.astype(jnp.bfloat16)
        rest = highest - max_hi.astype(jnp.float32)
        max_mid = rest.astype(jnp.bfloat16)
        max_lo = (rest - max_mid.astype(jnp.float32)).astype(jnp.bfloat16)
        stats = jnp.stack(
            [
                jnp.concatenate([max_hi, totals.reshape(QUERY_HEADS, draft_tree).astype(jnp.bfloat16)], axis=-1),
                jnp.concatenate([max_mid, max_lo], axis=-1),
            ],
            axis=1,
        )
        return jnp.concatenate(
            [blended.reshape(QUERY_HEADS, draft_tree, HEAD_SIZE).astype(jnp.bfloat16), stats], axis=1
        )

    packed = lax.map(cache_part, (query_block, cache_k, value_cache, cache_len))
    packed = packed.reshape(request_list, row_count, heads_dev, draft_tree + 2, HEAD_SIZE)
    gathered = lax.all_to_all(packed, "row", 1, 1).astype(jnp.float32)
    block_blend = gathered[:, :, :, :draft_tree, :]
    block_max = (
        gathered[:, :, :, draft_tree, :draft_tree] + gathered[:, :, :, draft_tree + 1, :draft_tree]
    ) + gathered[:, :, :, draft_tree + 1, draft_tree : 2 * draft_tree]
    block_total = gathered[:, :, :, draft_tree, draft_tree : 2 * draft_tree]
    allowed = ancestors(parents)[:, None, :, :]
    query_heads = projected_output[:, : QUERY_HEADS * HEAD_SIZE].reshape(
        request_list, draft_tree, QUERY_HEADS, HEAD_SIZE
    )
    query_own = lax.dynamic_slice_in_dim(query_heads, row_index * heads_dev, heads_dev, 2)
    key_own = lax.dynamic_slice_in_dim(
        jnp.repeat(new_key_block, head_groups, axis=2), row_index * heads_dev, heads_dev, 2
    )
    value_own = lax.dynamic_slice_in_dim(
        jnp.repeat(new_value_block, head_groups, axis=2), row_index * heads_dev, heads_dev, 2
    )
    tree_scores = (
        jnp.einsum("rthd,rshd->rhts", query_own, key_own, preferred_element_type=jnp.float32)
        * score_scale
    )
    tree_scores = jnp.where(allowed, tree_scores, masked_score)
    tree_max = jnp.max(tree_scores, axis=-1)
    tree_weights = jnp.where(allowed, jnp.exp(tree_scores - tree_max[..., None]), 0.0)
    tree_total = jnp.sum(tree_weights, axis=-1)
    tree_blend = jnp.einsum(
        "rhts,rshd->rhtd",
        tree_weights.astype(jnp.bfloat16),
        value_own,
        preferred_element_type=jnp.float32,
    )
    joint_max = jnp.maximum(jnp.max(block_max, axis=1), tree_max)
    block_scale = jnp.exp(block_max - joint_max[:, None])
    tree_scale = jnp.exp(tree_max - joint_max)
    numerator = jnp.sum(block_blend * block_scale[..., None], axis=1) + tree_blend * tree_scale[..., None]
    denominator = jnp.sum(block_total * block_scale, axis=1) + tree_total * tree_scale
    attended = (numerator / denominator[..., None]).astype(jnp.bfloat16)
    attended = attended.transpose(0, 2, 1, 3).reshape(rows_here, heads_dev * HEAD_SIZE)
    partial_out = jnp.dot(
        attended,
        lax.all_gather(w_out, "col", axis=1, tiled=True),
        preferred_element_type=jnp.float32,
    )
    return row_reduce(partial_out, "row", jnp.bfloat16).astype(jnp.bfloat16)


def solution(mesh):
    placed = (
        P("col", "row"),
        P("row"),
        P("row", "col"),
        P("row", "col"),
        P("col", "row", None),
        P("col", "row", None),
        P("col"),
        P("col", None),
    )
    return jax.shard_map(
        shards, mesh=mesh, in_specs=placed, out_specs=P("col", "row"), check_vma=False
    )
```

```python
import jax
import jax.numpy as jnp
from jax import lax
from jax.sharding import PartitionSpec as P

D = 4096
QUERY_HEADS = 32
KEY_VALUE_HEADS = 8
HEAD_SIZE = 128


masked_score = -1e30


def ancestors(parents):
    draft_tree = parents.shape[1]
    slot_ids = jnp.arange(draft_tree, dtype=jnp.int32)
    parent_links = (parents[:, :, None] == slot_ids[None, None, :]).astype(jnp.float32)
    reachable = parent_links + jnp.eye(draft_tree, dtype=jnp.float32)[None]
    for squaring in range(max(1, (draft_tree - 1).bit_length())):
        product = jnp.einsum("rij,rjk->rik", reachable, reachable, precision=lax.Precision.HIGHEST)
        reachable = (product > 0.5).astype(jnp.float32)
    return reachable > 0.5


def row_reduce(partial, axis_name, sent=jnp.float32):
    count = lax.axis_size(axis_name)
    rows, cols = partial.shape
    pieces = partial.reshape(rows, count, cols // count).transpose(1, 0, 2).astype(sent)
    received = lax.all_to_all(pieces, axis_name, 0, 0)
    return jnp.sum(received.astype(jnp.float32), axis=0)


def row_gather(value, axis_name):
    count = lax.axis_size(axis_name)
    copies = jnp.broadcast_to(value[None], (count,) + value.shape)
    return lax.all_to_all(copies, axis_name, 0, 0)


def shards(hidden_in, norm_gain, w_qkv, w_out, cache_k, value_cache, cache_len, parents):
    rows_here = hidden_in.shape[0]
    request_list = cache_k.shape[0]
    token_positions = cache_k.shape[1]
    draft_tree = parents.shape[1]
    head_groups = QUERY_HEADS // KEY_VALUE_HEADS
    row_count = lax.axis_size("row")
    heads_dev = QUERY_HEADS // row_count
    row_index = lax.axis_index("row")
    score_scale = HEAD_SIZE ** (-0.5)
    features = hidden_in.astype(jnp.float32)
    squares = jnp.sum(row_gather(jnp.sum(features * features, axis=1), "row"), axis=0)
    row_scale = lax.rsqrt(squares / D + 1e-05)
    normed = (features * row_scale[:, None] * norm_gain.astype(jnp.float32)[None, :]).astype(
        jnp.bfloat16
    )
    partial_value = jnp.dot(
        normed, lax.all_gather(w_qkv, "col", axis=1, tiled=True), preferred_element_type=jnp.float32
    )
    summed = row_reduce(partial_value, "row").astype(jnp.bfloat16)
    projected_output = row_gather(summed, "row").transpose(1, 0, 2).reshape(rows_here, -1)
    query_block = projected_output[:, : QUERY_HEADS * HEAD_SIZE].reshape(
        request_list, draft_tree, KEY_VALUE_HEADS, head_groups, HEAD_SIZE
    )
    new_key_block = projected_output[
        :, QUERY_HEADS * HEAD_SIZE : (QUERY_HEADS + KEY_VALUE_HEADS) * HEAD_SIZE
    ].reshape(request_list, draft_tree, KEY_VALUE_HEADS, HEAD_SIZE)
    new_value_block = projected_output[:, (QUERY_HEADS + KEY_VALUE_HEADS) * HEAD_SIZE :].reshape(
        request_list, draft_tree, KEY_VALUE_HEADS, HEAD_SIZE
    )
    first_slot = row_index * token_positions
    slot_ids = first_slot + jnp.arange(token_positions, dtype=jnp.int32)

    def cache_part(request_item):
        query_rows, cached_key_rows, cached_value_rows, length = request_item
        key_row_block = cached_key_rows.reshape(token_positions, KEY_VALUE_HEADS, HEAD_SIZE)
        value_row_block = cached_value_rows.reshape(token_positions, KEY_VALUE_HEADS, HEAD_SIZE)
        scores = (
            jnp.einsum(
                "tkgd,pkd->kgtp", query_rows, key_row_block, preferred_element_type=jnp.float32
            )
            * score_scale
        )
        visible = (slot_ids < length)[None, None, None, :]
        scores = jnp.where(visible, scores, masked_score)
        highest = jnp.max(scores, axis=-1)
        weights = jnp.where(visible, jnp.exp(scores - highest[..., None]), 0.0)
        totals = jnp.sum(weights, axis=-1)
        blended = jnp.einsum(
            "kgtp,pkd->kgtd",
            weights.astype(jnp.bfloat16),
            value_row_block,
            preferred_element_type=jnp.float32,
        )
        stats = jnp.concatenate(
            [highest.reshape(QUERY_HEADS, draft_tree), totals.reshape(QUERY_HEADS, draft_tree)],
            axis=-1,
        )
        return jnp.concatenate(
            [blended.reshape(QUERY_HEADS, draft_tree, HEAD_SIZE), stats[:, None, :]], axis=1
        )

    packed = lax.map(cache_part, (query_block, cache_k, value_cache, cache_len))
    packed = packed.reshape(request_list, row_count, heads_dev, draft_tree + 1, HEAD_SIZE)
    gathered = lax.all_to_all(packed, "row", 1, 1)
    block_blend = gathered[:, :, :, :draft_tree, :]
    block_max = gathered[:, :, :, draft_tree, :draft_tree]
    block_total = gathered[:, :, :, draft_tree, draft_tree : 2 * draft_tree]
    allowed = ancestors(parents)[:, None, :, :]
    query_heads = projected_output[:, : QUERY_HEADS * HEAD_SIZE].reshape(
        request_list, draft_tree, QUERY_HEADS, HEAD_SIZE
    )
    query_own = lax.dynamic_slice_in_dim(query_heads, row_index * heads_dev, heads_dev, 2)
    key_own = lax.dynamic_slice_in_dim(
        jnp.repeat(new_key_block, head_groups, axis=2), row_index * heads_dev, heads_dev, 2
    )
    value_own = lax.dynamic_slice_in_dim(
        jnp.repeat(new_value_block, head_groups, axis=2), row_index * heads_dev, heads_dev, 2
    )
    tree_scores = (
        jnp.einsum("rthd,rshd->rhts", query_own, key_own, preferred_element_type=jnp.float32)
        * score_scale
    )
    tree_scores = jnp.where(allowed, tree_scores, masked_score)
    tree_max = jnp.max(tree_scores, axis=-1)
    tree_weights = jnp.where(allowed, jnp.exp(tree_scores - tree_max[..., None]), 0.0)
    tree_total = jnp.sum(tree_weights, axis=-1)
    tree_blend = jnp.einsum(
        "rhts,rshd->rhtd",
        tree_weights.astype(jnp.bfloat16),
        value_own,
        preferred_element_type=jnp.float32,
    )
    joint_max = jnp.maximum(jnp.max(block_max, axis=1), tree_max)
    block_scale = jnp.exp(block_max - joint_max[:, None])
    tree_scale = jnp.exp(tree_max - joint_max)
    numerator = jnp.sum(block_blend * block_scale[..., None], axis=1) + tree_blend * tree_scale[..., None]
    denominator = jnp.sum(block_total * block_scale, axis=1) + tree_total * tree_scale
    attended = (numerator / denominator[..., None]).astype(jnp.bfloat16)
    attended = attended.transpose(0, 2, 1, 3).reshape(rows_here, heads_dev * HEAD_SIZE)
    partial_out = jnp.dot(
        attended,
        lax.all_gather(w_out, "col", axis=1, tiled=True),
        preferred_element_type=jnp.float32,
    )
    return row_reduce(partial_out, "row", jnp.bfloat16).astype(jnp.bfloat16)


def solution(mesh):
    placed = (
        P("col", "row"),
        P("row"),
        P("row", "col"),
        P("row", "col"),
        P("col", "row", None),
        P("col", "row", None),
        P("col"),
        P("col", None),
    )
    return jax.shard_map(
        shards, mesh=mesh, in_specs=placed, out_specs=P("col", "row"), check_vma=False
    )
```

```python
import jax
import jax.numpy as jnp
from jax import lax
from jax.sharding import PartitionSpec as P

D = 4096
QUERY_HEADS = 32
KEY_VALUE_HEADS = 8
HEAD_SIZE = 128


masked_score = -1e30


def ancestors(parents):
    draft_tree = parents.shape[1]
    slot_ids = jnp.arange(draft_tree, dtype=jnp.int32)
    parent_links = (parents[:, :, None] == slot_ids[None, None, :]).astype(jnp.float32)
    reachable = parent_links + jnp.eye(draft_tree, dtype=jnp.float32)[None]
    for squaring in range(max(1, (draft_tree - 1).bit_length())):
        product = jnp.einsum("rij,rjk->rik", reachable, reachable, precision=lax.Precision.HIGHEST)
        reachable = (product > 0.5).astype(jnp.float32)
    return reachable > 0.5


def row_reduce(partial, axis_name, sent=jnp.float32):
    count = lax.axis_size(axis_name)
    rows, cols = partial.shape
    pieces = partial.reshape(rows, count, cols // count).transpose(1, 0, 2).astype(sent)
    received = lax.all_to_all(pieces, axis_name, 0, 0)
    return jnp.sum(received.astype(jnp.float32), axis=0)


def row_gather(value, axis_name):
    count = lax.axis_size(axis_name)
    copies = jnp.broadcast_to(value[None], (count,) + value.shape)
    return lax.all_to_all(copies, axis_name, 0, 0)


def shards(hidden_in, norm_gain, w_qkv, w_out, cache_k, value_cache, cache_len, parents):
    rows_here = hidden_in.shape[0]
    request_list = cache_k.shape[0]
    token_positions = cache_k.shape[1]
    draft_tree = parents.shape[1]
    head_groups = QUERY_HEADS // KEY_VALUE_HEADS
    row_count = lax.axis_size("row")
    heads_dev = QUERY_HEADS // row_count
    row_index = lax.axis_index("row")
    score_scale = HEAD_SIZE ** (-0.5)
    features = hidden_in.astype(jnp.float32)
    squares = jnp.sum(row_gather(jnp.sum(features * features, axis=1), "row"), axis=0)
    row_scale = lax.rsqrt(squares / D + 1e-05)
    normed = (features * row_scale[:, None] * norm_gain.astype(jnp.float32)[None, :]).astype(
        jnp.bfloat16
    )
    half = w_qkv.shape[1] // 2
    halves = []
    for part in (w_qkv[:, :half], w_qkv[:, half:]):
        partial_value = jnp.dot(
            normed, lax.all_gather(part, "col", axis=1, tiled=True), preferred_element_type=jnp.float32
        )
        halves.append(row_reduce(partial_value, "row"))
    summed = jnp.concatenate(halves, axis=1).astype(jnp.bfloat16)
    projected_output = row_gather(summed, "row").transpose(1, 0, 2).reshape(rows_here, -1)
    query_block = projected_output[:, : QUERY_HEADS * HEAD_SIZE].reshape(
        request_list, draft_tree, KEY_VALUE_HEADS, head_groups, HEAD_SIZE
    )
    new_key_block = projected_output[
        :, QUERY_HEADS * HEAD_SIZE : (QUERY_HEADS + KEY_VALUE_HEADS) * HEAD_SIZE
    ].reshape(request_list, draft_tree, KEY_VALUE_HEADS, HEAD_SIZE)
    new_value_block = projected_output[:, (QUERY_HEADS + KEY_VALUE_HEADS) * HEAD_SIZE :].reshape(
        request_list, draft_tree, KEY_VALUE_HEADS, HEAD_SIZE
    )
    first_slot = row_index * token_positions
    slot_ids = first_slot + jnp.arange(token_positions, dtype=jnp.int32)

    def cache_part(request_item):
        query_rows, cached_key_rows, cached_value_rows, length = request_item
        key_row_block = cached_key_rows.reshape(token_positions, KEY_VALUE_HEADS, HEAD_SIZE)
        value_row_block = cached_value_rows.reshape(token_positions, KEY_VALUE_HEADS, HEAD_SIZE)
        scores = (
            jnp.einsum(
                "tkgd,pkd->kgtp", query_rows, key_row_block, preferred_element_type=jnp.float32
            )
            * score_scale
        )
        visible = (slot_ids < length)[None, None, None, :]
        scores = jnp.where(visible, scores, masked_score)
        highest = jnp.max(scores, axis=-1)
        weights = jnp.where(visible, jnp.exp(scores - highest[..., None]), 0.0)
        totals = jnp.sum(weights, axis=-1)
        blended = jnp.einsum(
            "kgtp,pkd->kgtd",
            weights.astype(jnp.bfloat16),
            value_row_block,
            preferred_element_type=jnp.float32,
        )
        stats = jnp.concatenate(
            [highest.reshape(QUERY_HEADS, draft_tree), totals.reshape(QUERY_HEADS, draft_tree)],
            axis=-1,
        )
        return jnp.concatenate(
            [blended.reshape(QUERY_HEADS, draft_tree, HEAD_SIZE), stats[:, None, :]], axis=1
        )

    packed = lax.map(cache_part, (query_block, cache_k, value_cache, cache_len))
    packed = packed.reshape(request_list, row_count, heads_dev, draft_tree + 1, HEAD_SIZE)
    gathered = lax.all_to_all(packed, "row", 1, 1)
    block_blend = gathered[:, :, :, :draft_tree, :]
    block_max = gathered[:, :, :, draft_tree, :draft_tree]
    block_total = gathered[:, :, :, draft_tree, draft_tree : 2 * draft_tree]
    allowed = ancestors(parents)[:, None, :, :]
    query_heads = projected_output[:, : QUERY_HEADS * HEAD_SIZE].reshape(
        request_list, draft_tree, QUERY_HEADS, HEAD_SIZE
    )
    query_own = lax.dynamic_slice_in_dim(query_heads, row_index * heads_dev, heads_dev, 2)
    key_own = lax.dynamic_slice_in_dim(
        jnp.repeat(new_key_block, head_groups, axis=2), row_index * heads_dev, heads_dev, 2
    )
    value_own = lax.dynamic_slice_in_dim(
        jnp.repeat(new_value_block, head_groups, axis=2), row_index * heads_dev, heads_dev, 2
    )
    tree_scores = (
        jnp.einsum("rthd,rshd->rhts", query_own, key_own, preferred_element_type=jnp.float32)
        * score_scale
    )
    tree_scores = jnp.where(allowed, tree_scores, masked_score)
    tree_max = jnp.max(tree_scores, axis=-1)
    tree_weights = jnp.where(allowed, jnp.exp(tree_scores - tree_max[..., None]), 0.0)
    tree_total = jnp.sum(tree_weights, axis=-1)
    tree_blend = jnp.einsum(
        "rhts,rshd->rhtd",
        tree_weights.astype(jnp.bfloat16),
        value_own,
        preferred_element_type=jnp.float32,
    )
    joint_max = jnp.maximum(jnp.max(block_max, axis=1), tree_max)
    block_scale = jnp.exp(block_max - joint_max[:, None])
    tree_scale = jnp.exp(tree_max - joint_max)
    numerator = jnp.sum(block_blend * block_scale[..., None], axis=1) + tree_blend * tree_scale[..., None]
    denominator = jnp.sum(block_total * block_scale, axis=1) + tree_total * tree_scale
    attended = (numerator / denominator[..., None]).astype(jnp.bfloat16)
    attended = attended.transpose(0, 2, 1, 3).reshape(rows_here, heads_dev * HEAD_SIZE)
    partial_out = jnp.dot(
        attended,
        lax.all_gather(w_out, "col", axis=1, tiled=True),
        preferred_element_type=jnp.float32,
    )
    return row_reduce(partial_out, "row", jnp.bfloat16).astype(jnp.bfloat16)


def solution(mesh):
    placed = (
        P("col", "row"),
        P("row"),
        P("row", "col"),
        P("row", "col"),
        P("col", "row", None),
        P("col", "row", None),
        P("col"),
        P("col", None),
    )
    return jax.shard_map(
        shards, mesh=mesh, in_specs=placed, out_specs=P("col", "row"), check_vma=False
    )
```

```python
import jax
import jax.numpy as jnp
from jax import lax
from jax.sharding import PartitionSpec as P

D = 4096
QUERY_HEADS = 32
KEY_VALUE_HEADS = 8
HEAD_SIZE = 128


masked_score = -1e30


def ancestors(parents):
    draft_tree = parents.shape[1]
    slot_ids = jnp.arange(draft_tree, dtype=jnp.int32)
    parent_links = (parents[:, :, None] == slot_ids[None, None, :]).astype(jnp.float32)
    reachable = parent_links + jnp.eye(draft_tree, dtype=jnp.float32)[None]
    for squaring in range(max(1, (draft_tree - 1).bit_length())):
        product = jnp.einsum("rij,rjk->rik", reachable, reachable, precision=lax.Precision.HIGHEST)
        reachable = (product > 0.5).astype(jnp.float32)
    return reachable > 0.5


def row_reduce(partial, axis_name, sent=jnp.float32):
    count = lax.axis_size(axis_name)
    rows, cols = partial.shape
    pieces = partial.reshape(rows, count, cols // count).transpose(1, 0, 2).astype(sent)
    received = lax.all_to_all(pieces, axis_name, 0, 0)
    return jnp.sum(received.astype(jnp.float32), axis=0)


def row_gather(value, axis_name):
    count = lax.axis_size(axis_name)
    copies = jnp.broadcast_to(value[None], (count,) + value.shape)
    return lax.all_to_all(copies, axis_name, 0, 0)


def shards(hidden_in, norm_gain, w_qkv, w_out, cache_k, value_cache, cache_len, parents):
    rows_here = hidden_in.shape[0]
    request_list = cache_k.shape[0]
    token_positions = cache_k.shape[1]
    draft_tree = parents.shape[1]
    head_groups = QUERY_HEADS // KEY_VALUE_HEADS
    row_count = lax.axis_size("row")
    heads_dev = QUERY_HEADS // row_count
    row_index = lax.axis_index("row")
    score_scale = HEAD_SIZE ** (-0.5)
    features = hidden_in.astype(jnp.float32)
    squares = jnp.sum(row_gather(jnp.sum(features * features, axis=1), "row"), axis=0)
    row_scale = lax.rsqrt(squares / D + 1e-05)
    normed = (features * row_scale[:, None] * norm_gain.astype(jnp.float32)[None, :]).astype(
        jnp.bfloat16
    )
    partial_value = jnp.dot(
        normed, lax.all_gather(w_qkv, "col", axis=1, tiled=True), preferred_element_type=jnp.float32
    )
    query_cols = QUERY_HEADS * HEAD_SIZE
    query_part = partial_value[:, :query_cols].reshape(rows_here, row_count, -1)
    pair_part = (
        partial_value[:, query_cols:]
        .reshape(rows_here, 2, KEY_VALUE_HEADS, HEAD_SIZE)
        .transpose(0, 2, 1, 3)
        .reshape(rows_here, row_count, -1)
    )
    owned = jnp.concatenate([query_part, pair_part], axis=2).transpose(1, 0, 2)
    summed = jnp.sum(lax.all_to_all(owned, "row", 0, 0), axis=0).astype(jnp.bfloat16)
    query_mine = summed[:, : heads_dev * HEAD_SIZE]
    pair_mine = summed[:, heads_dev * HEAD_SIZE :]
    partner = [(i, i ^ 1) for i in range(row_count)]
    pair_theirs = lax.ppermute(pair_mine, "row", partner)
    is_key = row_index % 2 == 0
    key_mine = jnp.where(is_key, pair_mine, pair_theirs)
    value_mine = jnp.where(is_key, pair_theirs, pair_mine)
    all_queries = row_gather(query_mine, "row").transpose(1, 0, 2).reshape(rows_here, -1)
    query_block = all_queries.reshape(
        request_list, draft_tree, KEY_VALUE_HEADS, head_groups, HEAD_SIZE
    )
    first_slot = row_index * token_positions
    slot_ids = first_slot + jnp.arange(token_positions, dtype=jnp.int32)

    def cache_part(request_item):
        query_rows, cached_key_rows, cached_value_rows, length = request_item
        key_row_block = cached_key_rows.reshape(token_positions, KEY_VALUE_HEADS, HEAD_SIZE)
        value_row_block = cached_value_rows.reshape(token_positions, KEY_VALUE_HEADS, HEAD_SIZE)
        scores = (
            jnp.einsum(
                "tkgd,pkd->kgtp", query_rows, key_row_block, preferred_element_type=jnp.float32
            )
            * score_scale
        )
        visible = (slot_ids < length)[None, None, None, :]
        scores = jnp.where(visible, scores, masked_score)
        highest = jnp.max(scores, axis=-1)
        weights = jnp.where(visible, jnp.exp(scores - highest[..., None]), 0.0)
        totals = jnp.sum(weights, axis=-1)
        blended = jnp.einsum(
            "kgtp,pkd->kgtd",
            weights.astype(jnp.bfloat16),
            value_row_block,
            preferred_element_type=jnp.float32,
        )
        stats = jnp.concatenate(
            [highest.reshape(QUERY_HEADS, draft_tree), totals.reshape(QUERY_HEADS, draft_tree)],
            axis=-1,
        )
        return jnp.concatenate(
            [blended.reshape(QUERY_HEADS, draft_tree, HEAD_SIZE), stats[:, None, :]], axis=1
        )

    packed = lax.map(cache_part, (query_block, cache_k, value_cache, cache_len))
    packed = packed.reshape(request_list, row_count, heads_dev, draft_tree + 1, HEAD_SIZE)
    gathered = lax.all_to_all(packed, "row", 1, 1)
    block_blend = gathered[:, :, :, :draft_tree, :]
    block_max = gathered[:, :, :, draft_tree, :draft_tree]
    block_total = gathered[:, :, :, draft_tree, draft_tree : 2 * draft_tree]
    allowed = ancestors(parents)[:, None, :, :]
    query_own = query_mine.reshape(request_list, draft_tree, heads_dev, HEAD_SIZE)
    key_own = jnp.broadcast_to(
        key_mine.reshape(request_list, draft_tree, 1, HEAD_SIZE),
        (request_list, draft_tree, heads_dev, HEAD_SIZE),
    )
    value_own = jnp.broadcast_to(
        value_mine.reshape(request_list, draft_tree, 1, HEAD_SIZE),
        (request_list, draft_tree, heads_dev, HEAD_SIZE),
    )
    tree_scores = (
        jnp.einsum("rthd,rshd->rhts", query_own, key_own, preferred_element_type=jnp.float32)
        * score_scale
    )
    tree_scores = jnp.where(allowed, tree_scores, masked_score)
    tree_max = jnp.max(tree_scores, axis=-1)
    tree_weights = jnp.where(allowed, jnp.exp(tree_scores - tree_max[..., None]), 0.0)
    tree_total = jnp.sum(tree_weights, axis=-1)
    tree_blend = jnp.einsum(
        "rhts,rshd->rhtd",
        tree_weights.astype(jnp.bfloat16),
        value_own,
        preferred_element_type=jnp.float32,
    )
    joint_max = jnp.maximum(jnp.max(block_max, axis=1), tree_max)
    block_scale = jnp.exp(block_max - joint_max[:, None])
    tree_scale = jnp.exp(tree_max - joint_max)
    numerator = jnp.sum(block_blend * block_scale[..., None], axis=1) + tree_blend * tree_scale[..., None]
    denominator = jnp.sum(block_total * block_scale, axis=1) + tree_total * tree_scale
    attended = (numerator / denominator[..., None]).astype(jnp.bfloat16)
    attended = attended.transpose(0, 2, 1, 3).reshape(rows_here, heads_dev * HEAD_SIZE)
    partial_out = jnp.dot(
        attended,
        lax.all_gather(w_out, "col", axis=1, tiled=True),
        preferred_element_type=jnp.float32,
    )
    return row_reduce(partial_out, "row", jnp.bfloat16).astype(jnp.bfloat16)


def solution(mesh):
    placed = (
        P("col", "row"),
        P("row"),
        P("row", "col"),
        P("row", "col"),
        P("col", "row", None),
        P("col", "row", None),
        P("col"),
        P("col", None),
    )
    return jax.shard_map(
        shards, mesh=mesh, in_specs=placed, out_specs=P("col", "row"), check_vma=False
    )
```

```python
import jax
import jax.numpy as jnp
from jax import lax
from jax.sharding import PartitionSpec as P

D = 4096
QUERY_HEADS = 32
KEY_VALUE_HEADS = 8
HEAD_SIZE = 128


masked_score = -1e30


def ancestors(parents):
    draft_tree = parents.shape[1]
    slot_ids = jnp.arange(draft_tree, dtype=jnp.int32)
    parent_links = (parents[:, :, None] == slot_ids[None, None, :]).astype(jnp.float32)
    reachable = parent_links + jnp.eye(draft_tree, dtype=jnp.float32)[None]
    for squaring in range(max(1, (draft_tree - 1).bit_length())):
        product = jnp.einsum("rij,rjk->rik", reachable, reachable, precision=lax.Precision.HIGHEST)
        reachable = (product > 0.5).astype(jnp.float32)
    return reachable > 0.5


def row_reduce(partial, axis_name, sent=jnp.float32):
    count = lax.axis_size(axis_name)
    rows, cols = partial.shape
    pieces = partial.reshape(rows, count, cols // count).transpose(1, 0, 2).astype(sent)
    received = lax.all_to_all(pieces, axis_name, 0, 0)
    return jnp.sum(received.astype(jnp.float32), axis=0)


def row_gather(value, axis_name):
    count = lax.axis_size(axis_name)
    copies = jnp.broadcast_to(value[None], (count,) + value.shape)
    return lax.all_to_all(copies, axis_name, 0, 0)


def shards(hidden_in, norm_gain, w_qkv, w_out, cache_k, value_cache, cache_len, parents):
    rows_here = hidden_in.shape[0]
    request_list = cache_k.shape[0]
    token_positions = cache_k.shape[1]
    draft_tree = parents.shape[1]
    head_groups = QUERY_HEADS // KEY_VALUE_HEADS
    row_count = lax.axis_size("row")
    heads_dev = QUERY_HEADS // row_count
    row_index = lax.axis_index("row")
    score_scale = HEAD_SIZE ** (-0.5)
    features = hidden_in.astype(jnp.float32)
    squares = jnp.sum(row_gather(jnp.sum(features * features, axis=1), "row"), axis=0)
    row_scale = lax.rsqrt(squares / D + 1e-05)
    normed = (features * row_scale[:, None] * norm_gain.astype(jnp.float32)[None, :]).astype(
        jnp.bfloat16
    )
    partial_value = jnp.dot(
        normed, lax.all_gather(w_qkv, "col", axis=1, tiled=True), preferred_element_type=jnp.float32
    )
    query_cols = QUERY_HEADS * HEAD_SIZE
    query_part = partial_value[:, :query_cols].reshape(rows_here, row_count, -1)
    pair_part = (
        partial_value[:, query_cols:]
        .reshape(rows_here, 2, KEY_VALUE_HEADS, HEAD_SIZE)
        .transpose(0, 2, 1, 3)
        .reshape(rows_here, row_count, -1)
    )
    owned = jnp.concatenate([query_part, pair_part], axis=2).transpose(1, 0, 2)
    summed = jnp.sum(lax.all_to_all(owned, "row", 0, 0), axis=0).astype(jnp.bfloat16)
    query_mine = summed[:, : heads_dev * HEAD_SIZE]
    pair_mine = summed[:, heads_dev * HEAD_SIZE :]
    partner = [(i, i ^ 1) for i in range(row_count)]
    pair_theirs = lax.ppermute(pair_mine, "row", partner)
    query_mine, pair_theirs = lax.optimization_barrier((query_mine, pair_theirs))
    is_key = row_index % 2 == 0
    key_mine = jnp.where(is_key, pair_mine, pair_theirs)
    value_mine = jnp.where(is_key, pair_theirs, pair_mine)
    all_queries = row_gather(query_mine, "row").transpose(1, 0, 2).reshape(rows_here, -1)
    query_block = all_queries.reshape(
        request_list, draft_tree, KEY_VALUE_HEADS, head_groups, HEAD_SIZE
    )
    first_slot = row_index * token_positions
    slot_ids = first_slot + jnp.arange(token_positions, dtype=jnp.int32)

    def cache_part(request_item):
        query_rows, cached_key_rows, cached_value_rows, length = request_item
        key_row_block = cached_key_rows.reshape(token_positions, KEY_VALUE_HEADS, HEAD_SIZE)
        value_row_block = cached_value_rows.reshape(token_positions, KEY_VALUE_HEADS, HEAD_SIZE)
        scores = (
            jnp.einsum(
                "tkgd,pkd->kgtp", query_rows, key_row_block, preferred_element_type=jnp.float32
            )
            * score_scale
        )
        visible = (slot_ids < length)[None, None, None, :]
        scores = jnp.where(visible, scores, masked_score)
        highest = jnp.max(scores, axis=-1)
        weights = jnp.where(visible, jnp.exp(scores - highest[..., None]), 0.0)
        totals = jnp.sum(weights, axis=-1)
        blended = jnp.einsum(
            "kgtp,pkd->kgtd",
            weights.astype(jnp.bfloat16),
            value_row_block,
            preferred_element_type=jnp.float32,
        )
        stats = jnp.concatenate(
            [highest.reshape(QUERY_HEADS, draft_tree), totals.reshape(QUERY_HEADS, draft_tree)],
            axis=-1,
        )
        return jnp.concatenate(
            [blended.reshape(QUERY_HEADS, draft_tree, HEAD_SIZE), stats[:, None, :]], axis=1
        )

    packed = lax.map(cache_part, (query_block, cache_k, value_cache, cache_len))
    packed = packed.reshape(request_list, row_count, heads_dev, draft_tree + 1, HEAD_SIZE)
    gathered = lax.all_to_all(packed, "row", 1, 1)
    block_blend = gathered[:, :, :, :draft_tree, :]
    block_max = gathered[:, :, :, draft_tree, :draft_tree]
    block_total = gathered[:, :, :, draft_tree, draft_tree : 2 * draft_tree]
    allowed = ancestors(parents)[:, None, :, :]
    query_own = query_mine.reshape(request_list, draft_tree, heads_dev, HEAD_SIZE)
    key_own = jnp.broadcast_to(
        key_mine.reshape(request_list, draft_tree, 1, HEAD_SIZE),
        (request_list, draft_tree, heads_dev, HEAD_SIZE),
    )
    value_own = jnp.broadcast_to(
        value_mine.reshape(request_list, draft_tree, 1, HEAD_SIZE),
        (request_list, draft_tree, heads_dev, HEAD_SIZE),
    )
    tree_scores = (
        jnp.einsum("rthd,rshd->rhts", query_own, key_own, preferred_element_type=jnp.float32)
        * score_scale
    )
    tree_scores = jnp.where(allowed, tree_scores, masked_score)
    tree_max = jnp.max(tree_scores, axis=-1)
    tree_weights = jnp.where(allowed, jnp.exp(tree_scores - tree_max[..., None]), 0.0)
    tree_total = jnp.sum(tree_weights, axis=-1)
    tree_blend = jnp.einsum(
        "rhts,rshd->rhtd",
        tree_weights.astype(jnp.bfloat16),
        value_own,
        preferred_element_type=jnp.float32,
    )
    joint_max = jnp.maximum(jnp.max(block_max, axis=1), tree_max)
    block_scale = jnp.exp(block_max - joint_max[:, None])
    tree_scale = jnp.exp(tree_max - joint_max)
    numerator = jnp.sum(block_blend * block_scale[..., None], axis=1) + tree_blend * tree_scale[..., None]
    denominator = jnp.sum(block_total * block_scale, axis=1) + tree_total * tree_scale
    attended = (numerator / denominator[..., None]).astype(jnp.bfloat16)
    attended = attended.transpose(0, 2, 1, 3).reshape(rows_here, heads_dev * HEAD_SIZE)
    partial_out = jnp.dot(
        attended,
        lax.all_gather(w_out, "col", axis=1, tiled=True),
        preferred_element_type=jnp.float32,
    )
    return row_reduce(partial_out, "row", jnp.bfloat16).astype(jnp.bfloat16)


def solution(mesh):
    placed = (
        P("col", "row"),
        P("row"),
        P("row", "col"),
        P("row", "col"),
        P("col", "row", None),
        P("col", "row", None),
        P("col"),
        P("col", None),
    )
    return jax.shard_map(
        shards, mesh=mesh, in_specs=placed, out_specs=P("col", "row"), check_vma=False
    )
```

```python
import jax
import jax.numpy as jnp
from jax import lax
from jax.sharding import PartitionSpec as P

D = 4096
QUERY_HEADS = 32
KEY_VALUE_HEADS = 8
HEAD_SIZE = 128


masked_score = -1e30


def ancestors(parents):
    draft_tree = parents.shape[1]
    slot_ids = jnp.arange(draft_tree, dtype=jnp.int32)
    parent_links = (parents[:, :, None] == slot_ids[None, None, :]).astype(jnp.float32)
    reachable = parent_links + jnp.eye(draft_tree, dtype=jnp.float32)[None]
    for squaring in range(max(1, (draft_tree - 1).bit_length())):
        product = jnp.einsum("rij,rjk->rik", reachable, reachable, precision=lax.Precision.HIGHEST)
        reachable = (product > 0.5).astype(jnp.float32)
    return reachable > 0.5


def row_reduce(partial, axis_name, sent=jnp.float32):
    count = lax.axis_size(axis_name)
    rows, cols = partial.shape
    pieces = partial.reshape(rows, count, cols // count).transpose(1, 0, 2).astype(sent)
    received = lax.all_to_all(pieces, axis_name, 0, 0)
    return jnp.sum(received.astype(jnp.float32), axis=0)


def row_gather(value, axis_name):
    count = lax.axis_size(axis_name)
    copies = jnp.broadcast_to(value[None], (count,) + value.shape)
    return lax.all_to_all(copies, axis_name, 0, 0)


def shards(hidden_in, norm_gain, w_qkv, w_out, cache_k, value_cache, cache_len, parents):
    rows_here = hidden_in.shape[0]
    request_list = cache_k.shape[0]
    token_positions = cache_k.shape[1]
    draft_tree = parents.shape[1]
    head_groups = QUERY_HEADS // KEY_VALUE_HEADS
    row_count = lax.axis_size("row")
    heads_dev = QUERY_HEADS // row_count
    row_index = lax.axis_index("row")
    score_scale = HEAD_SIZE ** (-0.5)
    features = hidden_in.astype(jnp.float32)
    squares = jnp.sum(row_gather(jnp.sum(features * features, axis=1), "row"), axis=0)
    row_scale = lax.rsqrt(squares / D + 1e-05)
    normed = (features * row_scale[:, None] * norm_gain.astype(jnp.float32)[None, :]).astype(
        jnp.bfloat16
    )
    partial_value = jnp.dot(
        normed, lax.all_gather(w_qkv, "col", axis=1, tiled=True), preferred_element_type=jnp.float32
    )
    query_cols = QUERY_HEADS * HEAD_SIZE
    query_part = partial_value[:, :query_cols].reshape(rows_here, row_count, -1)
    pair_part = (
        partial_value[:, query_cols:]
        .reshape(rows_here, 2, KEY_VALUE_HEADS, HEAD_SIZE)
        .transpose(0, 2, 1, 3)
        .reshape(rows_here, row_count, -1)
    )
    owned = jnp.concatenate([query_part, pair_part], axis=2).transpose(1, 0, 2)
    summed = jnp.sum(lax.all_to_all(owned, "row", 0, 0), axis=0).astype(jnp.bfloat16)
    query_mine = summed[:, : heads_dev * HEAD_SIZE]
    pair_mine = summed[:, heads_dev * HEAD_SIZE :]
    partner = [(i, i ^ 1) for i in range(row_count)]
    pair_theirs = lax.ppermute(pair_mine, "row", partner)
    is_key = row_index % 2 == 0
    key_mine = jnp.where(is_key, pair_mine, pair_theirs)
    value_mine = jnp.where(is_key, pair_theirs, pair_mine)
    all_queries = row_gather(query_mine, "row").transpose(1, 0, 2).reshape(rows_here, -1)
    query_block = all_queries.reshape(
        request_list, draft_tree, KEY_VALUE_HEADS, head_groups, HEAD_SIZE
    )
    first_slot = row_index * token_positions
    slot_ids = first_slot + jnp.arange(token_positions, dtype=jnp.int32)

    def cache_part(request_item):
        query_rows, cached_key_rows, cached_value_rows, length = request_item
        key_row_block = cached_key_rows.reshape(token_positions, KEY_VALUE_HEADS, HEAD_SIZE)
        value_row_block = cached_value_rows.reshape(token_positions, KEY_VALUE_HEADS, HEAD_SIZE)
        scores = (
            jnp.einsum(
                "tkgd,pkd->kgtp", query_rows, key_row_block, preferred_element_type=jnp.float32
            )
            * score_scale
        )
        visible = (slot_ids < length)[None, None, None, :]
        scores = jnp.where(visible, scores, masked_score)
        highest = jnp.max(scores, axis=-1)
        weights = jnp.where(visible, jnp.exp(scores - highest[..., None]), 0.0)
        totals = jnp.sum(weights, axis=-1)
        blended = jnp.einsum(
            "kgtp,pkd->kgtd",
            weights.astype(jnp.bfloat16),
            value_row_block,
            preferred_element_type=jnp.float32,
        )
        stats = jnp.concatenate(
            [highest.reshape(QUERY_HEADS, draft_tree), totals.reshape(QUERY_HEADS, draft_tree)],
            axis=-1,
        )
        return blended.reshape(QUERY_HEADS, draft_tree, HEAD_SIZE).astype(jnp.bfloat16), stats

    blends, stats = lax.map(cache_part, (query_block, cache_k, value_cache, cache_len))
    blends = blends.reshape(request_list, row_count, heads_dev, draft_tree, HEAD_SIZE)
    stats = stats.reshape(request_list, row_count, heads_dev, 2 * draft_tree)
    block_blend = lax.all_to_all(blends, "row", 1, 1).astype(jnp.float32)
    stats = lax.all_to_all(stats, "row", 1, 1)
    block_max = stats[..., :draft_tree]
    block_total = stats[..., draft_tree:]
    allowed = ancestors(parents)[:, None, :, :]
    query_own = query_mine.reshape(request_list, draft_tree, heads_dev, HEAD_SIZE)
    key_own = jnp.broadcast_to(
        key_mine.reshape(request_list, draft_tree, 1, HEAD_SIZE),
        (request_list, draft_tree, heads_dev, HEAD_SIZE),
    )
    value_own = jnp.broadcast_to(
        value_mine.reshape(request_list, draft_tree, 1, HEAD_SIZE),
        (request_list, draft_tree, heads_dev, HEAD_SIZE),
    )
    tree_scores = (
        jnp.einsum("rthd,rshd->rhts", query_own, key_own, preferred_element_type=jnp.float32)
        * score_scale
    )
    tree_scores = jnp.where(allowed, tree_scores, masked_score)
    tree_max = jnp.max(tree_scores, axis=-1)
    tree_weights = jnp.where(allowed, jnp.exp(tree_scores - tree_max[..., None]), 0.0)
    tree_total = jnp.sum(tree_weights, axis=-1)
    tree_blend = jnp.einsum(
        "rhts,rshd->rhtd",
        tree_weights.astype(jnp.bfloat16),
        value_own,
        preferred_element_type=jnp.float32,
    )
    joint_max = jnp.maximum(jnp.max(block_max, axis=1), tree_max)
    block_scale = jnp.exp(block_max - joint_max[:, None])
    tree_scale = jnp.exp(tree_max - joint_max)
    numerator = jnp.sum(block_blend * block_scale[..., None], axis=1) + tree_blend * tree_scale[..., None]
    denominator = jnp.sum(block_total * block_scale, axis=1) + tree_total * tree_scale
    attended = (numerator / denominator[..., None]).astype(jnp.bfloat16)
    attended = attended.transpose(0, 2, 1, 3).reshape(rows_here, heads_dev * HEAD_SIZE)
    partial_out = jnp.dot(
        attended,
        lax.all_gather(w_out, "col", axis=1, tiled=True),
        preferred_element_type=jnp.float32,
    )
    return row_reduce(partial_out, "row", jnp.bfloat16).astype(jnp.bfloat16)


def solution(mesh):
    placed = (
        P("col", "row"),
        P("row"),
        P("row", "col"),
        P("row", "col"),
        P("col", "row", None),
        P("col", "row", None),
        P("col"),
        P("col", None),
    )
    return jax.shard_map(
        shards, mesh=mesh, in_specs=placed, out_specs=P("col", "row"), check_vma=False
    )
```

```python
import jax
import jax.numpy as jnp
from jax import lax
from jax.sharding import PartitionSpec as P

D = 4096
QUERY_HEADS = 32
KEY_VALUE_HEADS = 8
HEAD_SIZE = 128


masked_score = -1e30


def ancestors(parents):
    draft_tree = parents.shape[1]
    slot_ids = jnp.arange(draft_tree, dtype=jnp.int32)
    parent_links = (parents[:, :, None] == slot_ids[None, None, :]).astype(jnp.float32)
    reachable = parent_links + jnp.eye(draft_tree, dtype=jnp.float32)[None]
    for squaring in range(max(1, (draft_tree - 1).bit_length())):
        product = jnp.einsum("rij,rjk->rik", reachable, reachable, precision=lax.Precision.HIGHEST)
        reachable = (product > 0.5).astype(jnp.float32)
    return reachable > 0.5


def row_reduce(partial, axis_name, sent=jnp.float32):
    count = lax.axis_size(axis_name)
    rows, cols = partial.shape
    pieces = partial.reshape(rows, count, cols // count).transpose(1, 0, 2).astype(sent)
    received = lax.all_to_all(pieces, axis_name, 0, 0)
    return jnp.sum(received.astype(jnp.float32), axis=0)


def row_gather(value, axis_name):
    count = lax.axis_size(axis_name)
    copies = jnp.broadcast_to(value[None], (count,) + value.shape)
    return lax.all_to_all(copies, axis_name, 0, 0)


def shards(hidden_in, norm_gain, w_qkv, w_out, cache_k, value_cache, cache_len, parents):
    rows_here = hidden_in.shape[0]
    request_list = cache_k.shape[0]
    token_positions = cache_k.shape[1]
    draft_tree = parents.shape[1]
    head_groups = QUERY_HEADS // KEY_VALUE_HEADS
    row_count = lax.axis_size("row")
    heads_dev = QUERY_HEADS // row_count
    row_index = lax.axis_index("row")
    score_scale = HEAD_SIZE ** (-0.5)
    features = hidden_in.astype(jnp.float32)
    squares = jnp.sum(row_gather(jnp.sum(features * features, axis=1), "row"), axis=0)
    row_scale = lax.rsqrt(squares / D + 1e-05)
    normed = (features * row_scale[:, None] * norm_gain.astype(jnp.float32)[None, :]).astype(
        jnp.bfloat16
    )
    partial_value = jnp.dot(
        normed, lax.all_gather(w_qkv, "col", axis=1, tiled=True), preferred_element_type=jnp.float32
    )
    query_cols = QUERY_HEADS * HEAD_SIZE
    query_part = partial_value[:, :query_cols].reshape(rows_here, row_count, -1)
    pair_part = (
        partial_value[:, query_cols:]
        .reshape(rows_here, 2, KEY_VALUE_HEADS, HEAD_SIZE)
        .transpose(0, 2, 1, 3)
        .reshape(rows_here, row_count, -1)
    )
    owned = jnp.concatenate([query_part, pair_part], axis=2).transpose(1, 0, 2)
    summed = jnp.sum(lax.all_to_all(owned, "row", 0, 0), axis=0).astype(jnp.bfloat16)
    query_mine = summed[:, : heads_dev * HEAD_SIZE]
    pair_mine = summed[:, heads_dev * HEAD_SIZE :]
    partner = [(i, i ^ 1) for i in range(row_count)]
    pair_theirs = lax.ppermute(pair_mine, "row", partner)
    is_key = row_index % 2 == 0
    key_mine = jnp.where(is_key, pair_mine, pair_theirs)
    value_mine = jnp.where(is_key, pair_theirs, pair_mine)
    def by_head(cache):
        local = cache.reshape(token_positions, KEY_VALUE_HEADS, HEAD_SIZE).transpose(1, 0, 2)
        pieces = jnp.repeat(local, row_count // KEY_VALUE_HEADS, axis=0)
        return lax.all_to_all(pieces, "row", 0, 0).reshape(row_count * token_positions, HEAD_SIZE)

    keys = by_head(cache_k[0])
    values = by_head(value_cache[0])
    window = row_count * token_positions
    query_own = query_mine.reshape(draft_tree, heads_dev, HEAD_SIZE)
    scores = (
        jnp.einsum("thd,pd->htp", query_own, keys, preferred_element_type=jnp.float32)
        * score_scale
    )
    visible = (jnp.arange(window, dtype=jnp.int32) < cache_len[0])[None, None, :]
    scores = jnp.where(visible, scores, masked_score)
    allowed = ancestors(parents)[0][None, :, :]
    tree_scores = (
        jnp.einsum("thd,sd->hts", query_own, key_mine, preferred_element_type=jnp.float32)
        * score_scale
    )
    tree_scores = jnp.where(allowed, tree_scores, masked_score)
    highest = jnp.maximum(jnp.max(scores, axis=-1), jnp.max(tree_scores, axis=-1))
    weights = jnp.where(visible, jnp.exp(scores - highest[..., None]), 0.0)
    tree_weights = jnp.where(allowed, jnp.exp(tree_scores - highest[..., None]), 0.0)
    totals = jnp.sum(weights, axis=-1) + jnp.sum(tree_weights, axis=-1)
    blended = jnp.einsum(
        "htp,pd->htd", weights.astype(jnp.bfloat16), values, preferred_element_type=jnp.float32
    ) + jnp.einsum(
        "hts,sd->htd", tree_weights.astype(jnp.bfloat16), value_mine, preferred_element_type=jnp.float32
    )
    attended = (blended / totals[..., None]).astype(jnp.bfloat16)
    attended = attended.transpose(1, 0, 2).reshape(rows_here, heads_dev * HEAD_SIZE)
    partial_out = jnp.dot(
        attended,
        lax.all_gather(w_out, "col", axis=1, tiled=True),
        preferred_element_type=jnp.float32,
    )
    return row_reduce(partial_out, "row", jnp.bfloat16).astype(jnp.bfloat16)


def solution(mesh):
    placed = (
        P("col", "row"),
        P("row"),
        P("row", "col"),
        P("row", "col"),
        P("col", "row", None),
        P("col", "row", None),
        P("col"),
        P("col", None),
    )
    return jax.shard_map(
        shards, mesh=mesh, in_specs=placed, out_specs=P("col", "row"), check_vma=False
    )
```

```python
import jax
import jax.numpy as jnp
from jax import lax
from jax.sharding import PartitionSpec as P

D = 4096
QUERY_HEADS = 32
KEY_VALUE_HEADS = 8
HEAD_SIZE = 128


masked_score = -1e30


def ancestors(parents):
    draft_tree = parents.shape[1]
    slot_ids = jnp.arange(draft_tree, dtype=jnp.int32)
    parent_links = (parents[:, :, None] == slot_ids[None, None, :]).astype(jnp.float32)
    reachable = parent_links + jnp.eye(draft_tree, dtype=jnp.float32)[None]
    for squaring in range(max(1, (draft_tree - 1).bit_length())):
        product = jnp.einsum("rij,rjk->rik", reachable, reachable, precision=lax.Precision.HIGHEST)
        reachable = (product > 0.5).astype(jnp.float32)
    return reachable > 0.5


def row_reduce(partial, axis_name, sent=jnp.float32):
    count = lax.axis_size(axis_name)
    rows, cols = partial.shape
    pieces = partial.reshape(rows, count, cols // count).transpose(1, 0, 2).astype(sent)
    received = lax.all_to_all(pieces, axis_name, 0, 0)
    return jnp.sum(received.astype(jnp.float32), axis=0)


def row_gather(value, axis_name):
    count = lax.axis_size(axis_name)
    copies = jnp.broadcast_to(value[None], (count,) + value.shape)
    return lax.all_to_all(copies, axis_name, 0, 0)


def shards(hidden_in, norm_gain, w_qkv, w_out, cache_k, value_cache, cache_len, parents):
    rows_here = hidden_in.shape[0]
    request_list = cache_k.shape[0]
    token_positions = cache_k.shape[1]
    draft_tree = parents.shape[1]
    head_groups = QUERY_HEADS // KEY_VALUE_HEADS
    row_count = lax.axis_size("row")
    heads_dev = QUERY_HEADS // row_count
    row_index = lax.axis_index("row")
    score_scale = HEAD_SIZE ** (-0.5)
    features = hidden_in.astype(jnp.float32)
    squares = jnp.sum(row_gather(jnp.sum(features * features, axis=1), "row"), axis=0)
    row_scale = lax.rsqrt(squares / D + 1e-05)
    normed = (features * row_scale[:, None] * norm_gain.astype(jnp.float32)[None, :]).astype(
        jnp.bfloat16
    )
    partial_value = jnp.dot(
        normed, lax.all_gather(w_qkv, "col", axis=1, tiled=True), preferred_element_type=jnp.float32
    )
    local = jnp.stack([cache_k[0], value_cache[0]]).reshape(
        2, token_positions, KEY_VALUE_HEADS, HEAD_SIZE
    ).transpose(2, 0, 1, 3)
    pieces = jnp.repeat(local, row_count // KEY_VALUE_HEADS, axis=0)
    by_head = lax.all_to_all(pieces, "row", 0, 0)
    by_head, partial_value = lax.optimization_barrier((by_head, partial_value))
    keys = by_head[:, 0].reshape(row_count * token_positions, HEAD_SIZE)
    values = by_head[:, 1].reshape(row_count * token_positions, HEAD_SIZE)
    query_cols = QUERY_HEADS * HEAD_SIZE
    query_part = partial_value[:, :query_cols].reshape(rows_here, row_count, -1)
    pair_part = (
        partial_value[:, query_cols:]
        .reshape(rows_here, 2, KEY_VALUE_HEADS, HEAD_SIZE)
        .transpose(0, 2, 1, 3)
        .reshape(rows_here, row_count, -1)
    )
    owned = jnp.concatenate([query_part, pair_part], axis=2).transpose(1, 0, 2)
    summed = jnp.sum(lax.all_to_all(owned, "row", 0, 0), axis=0).astype(jnp.bfloat16)
    query_mine = summed[:, : heads_dev * HEAD_SIZE]
    pair_mine = summed[:, heads_dev * HEAD_SIZE :]
    partner = [(i, i ^ 1) for i in range(row_count)]
    pair_theirs = lax.ppermute(pair_mine, "row", partner)
    is_key = row_index % 2 == 0
    key_mine = jnp.where(is_key, pair_mine, pair_theirs)
    value_mine = jnp.where(is_key, pair_theirs, pair_mine)
    window = row_count * token_positions
    query_own = query_mine.reshape(draft_tree, heads_dev, HEAD_SIZE)
    scores = (
        jnp.einsum("thd,pd->htp", query_own, keys, preferred_element_type=jnp.float32)
        * score_scale
    )
    visible = (jnp.arange(window, dtype=jnp.int32) < cache_len[0])[None, None, :]
    scores = jnp.where(visible, scores, masked_score)
    allowed = ancestors(parents)[0][None, :, :]
    tree_scores = (
        jnp.einsum("thd,sd->hts", query_own, key_mine, preferred_element_type=jnp.float32)
        * score_scale
    )
    tree_scores = jnp.where(allowed, tree_scores, masked_score)
    highest = jnp.maximum(jnp.max(scores, axis=-1), jnp.max(tree_scores, axis=-1))
    weights = jnp.where(visible, jnp.exp(scores - highest[..., None]), 0.0)
    tree_weights = jnp.where(allowed, jnp.exp(tree_scores - highest[..., None]), 0.0)
    totals = jnp.sum(weights, axis=-1) + jnp.sum(tree_weights, axis=-1)
    blended = jnp.einsum(
        "htp,pd->htd", weights.astype(jnp.bfloat16), values, preferred_element_type=jnp.float32
    ) + jnp.einsum(
        "hts,sd->htd", tree_weights.astype(jnp.bfloat16), value_mine, preferred_element_type=jnp.float32
    )
    attended = (blended / totals[..., None]).astype(jnp.bfloat16)
    attended = attended.transpose(1, 0, 2).reshape(rows_here, heads_dev * HEAD_SIZE)
    partial_out = jnp.dot(
        attended,
        lax.all_gather(w_out, "col", axis=1, tiled=True),
        preferred_element_type=jnp.float32,
    )
    return row_reduce(partial_out, "row", jnp.bfloat16).astype(jnp.bfloat16)


def solution(mesh):
    placed = (
        P("col", "row"),
        P("row"),
        P("row", "col"),
        P("row", "col"),
        P("col", "row", None),
        P("col", "row", None),
        P("col"),
        P("col", None),
    )
    return jax.shard_map(
        shards, mesh=mesh, in_specs=placed, out_specs=P("col", "row"), check_vma=False
    )
```

```python
import jax
import jax.numpy as jnp
from jax import lax
from jax.sharding import PartitionSpec as P

D = 4096
QUERY_HEADS = 32
KEY_VALUE_HEADS = 8
HEAD_SIZE = 128


masked_score = -1e30


def ancestors(parents):
    draft_tree = parents.shape[1]
    slot_ids = jnp.arange(draft_tree, dtype=jnp.int32)
    parent_links = (parents[:, :, None] == slot_ids[None, None, :]).astype(jnp.float32)
    reachable = parent_links + jnp.eye(draft_tree, dtype=jnp.float32)[None]
    for squaring in range(max(1, (draft_tree - 1).bit_length())):
        product = jnp.einsum("rij,rjk->rik", reachable, reachable, precision=lax.Precision.HIGHEST)
        reachable = (product > 0.5).astype(jnp.float32)
    return reachable > 0.5


def row_reduce(partial, axis_name, sent=jnp.float32):
    count = lax.axis_size(axis_name)
    rows, cols = partial.shape
    pieces = partial.reshape(rows, count, cols // count).transpose(1, 0, 2).astype(sent)
    received = lax.all_to_all(pieces, axis_name, 0, 0)
    return jnp.sum(received.astype(jnp.float32), axis=0)


def row_gather(value, axis_name):
    count = lax.axis_size(axis_name)
    copies = jnp.broadcast_to(value[None], (count,) + value.shape)
    return lax.all_to_all(copies, axis_name, 0, 0)


def shards(hidden_in, norm_gain, w_qkv, w_out, cache_k, value_cache, cache_len, parents):
    rows_here = hidden_in.shape[0]
    request_list = cache_k.shape[0]
    token_positions = cache_k.shape[1]
    draft_tree = parents.shape[1]
    head_groups = QUERY_HEADS // KEY_VALUE_HEADS
    row_count = lax.axis_size("row")
    heads_dev = QUERY_HEADS // row_count
    row_index = lax.axis_index("row")
    score_scale = HEAD_SIZE ** (-0.5)
    features = hidden_in.astype(jnp.float32)
    squares = jnp.sum(row_gather(jnp.sum(features * features, axis=1), "row"), axis=0)
    row_scale = lax.rsqrt(squares / D + 1e-05)
    normed = (features * row_scale[:, None] * norm_gain.astype(jnp.float32)[None, :]).astype(
        jnp.bfloat16
    )
    partial_value = jnp.dot(
        normed, lax.all_gather(w_qkv, "col", axis=1, tiled=True), preferred_element_type=jnp.float32
    )
    local = jnp.stack([cache_k[0], value_cache[0]]).reshape(
        2, token_positions, KEY_VALUE_HEADS, HEAD_SIZE
    ).transpose(2, 0, 1, 3)
    pieces = jnp.repeat(local, row_count // KEY_VALUE_HEADS, axis=0)
    by_head = lax.all_to_all(pieces, "row", 0, 0)
    by_head, partial_value = lax.optimization_barrier((by_head, partial_value))
    out_weights = row_gather(w_out, "col").transpose(1, 0, 2).reshape(w_out.shape[0], -1)
    out_weights, by_head = lax.optimization_barrier((out_weights, by_head))
    keys = by_head[:, 0].reshape(row_count * token_positions, HEAD_SIZE)
    values = by_head[:, 1].reshape(row_count * token_positions, HEAD_SIZE)
    query_cols = QUERY_HEADS * HEAD_SIZE
    query_part = partial_value[:, :query_cols].reshape(rows_here, row_count, -1)
    pair_part = (
        partial_value[:, query_cols:]
        .reshape(rows_here, 2, KEY_VALUE_HEADS, HEAD_SIZE)
        .transpose(0, 2, 1, 3)
        .reshape(rows_here, row_count, -1)
    )
    owned = jnp.concatenate([query_part, pair_part], axis=2).transpose(1, 0, 2)
    summed = jnp.sum(lax.all_to_all(owned, "row", 0, 0), axis=0).astype(jnp.bfloat16)
    query_mine = summed[:, : heads_dev * HEAD_SIZE]
    pair_mine = summed[:, heads_dev * HEAD_SIZE :]
    partner = [(i, i ^ 1) for i in range(row_count)]
    pair_theirs = lax.ppermute(pair_mine, "row", partner)
    is_key = row_index % 2 == 0
    key_mine = jnp.where(is_key, pair_mine, pair_theirs)
    value_mine = jnp.where(is_key, pair_theirs, pair_mine)
    window = row_count * token_positions
    query_own = query_mine.reshape(draft_tree, heads_dev, HEAD_SIZE)
    scores = (
        jnp.einsum("thd,pd->htp", query_own, keys, preferred_element_type=jnp.float32)
        * score_scale
    )
    visible = (jnp.arange(window, dtype=jnp.int32) < cache_len[0])[None, None, :]
    scores = jnp.where(visible, scores, masked_score)
    allowed = ancestors(parents)[0][None, :, :]
    tree_scores = (
        jnp.einsum("thd,sd->hts", query_own, key_mine, preferred_element_type=jnp.float32)
        * score_scale
    )
    tree_scores = jnp.where(allowed, tree_scores, masked_score)
    highest = jnp.maximum(jnp.max(scores, axis=-1), jnp.max(tree_scores, axis=-1))
    weights = jnp.where(visible, jnp.exp(scores - highest[..., None]), 0.0)
    tree_weights = jnp.where(allowed, jnp.exp(tree_scores - highest[..., None]), 0.0)
    totals = jnp.sum(weights, axis=-1) + jnp.sum(tree_weights, axis=-1)
    blended = jnp.einsum(
        "htp,pd->htd", weights.astype(jnp.bfloat16), values, preferred_element_type=jnp.float32
    ) + jnp.einsum(
        "hts,sd->htd", tree_weights.astype(jnp.bfloat16), value_mine, preferred_element_type=jnp.float32
    )
    attended = (blended / totals[..., None]).astype(jnp.bfloat16)
    attended = attended.transpose(1, 0, 2).reshape(rows_here, heads_dev * HEAD_SIZE)
    partial_out = jnp.dot(
        attended,
        out_weights,
        preferred_element_type=jnp.float32,
    )
    return row_reduce(partial_out, "row", jnp.bfloat16).astype(jnp.bfloat16)


def solution(mesh):
    placed = (
        P("col", "row"),
        P("row"),
        P("row", "col"),
        P("row", "col"),
        P("col", "row", None),
        P("col", "row", None),
        P("col"),
        P("col", None),
    )
    return jax.shard_map(
        shards, mesh=mesh, in_specs=placed, out_specs=P("col", "row"), check_vma=False
    )
```

```python
import jax
import jax.numpy as jnp
from jax import lax
from jax.sharding import PartitionSpec as P

D = 4096
QUERY_HEADS = 32
KEY_VALUE_HEADS = 8
HEAD_SIZE = 128


masked_score = -1e30


def ancestors(parents):
    draft_tree = parents.shape[1]
    slot_ids = jnp.arange(draft_tree, dtype=jnp.int32)
    parent_links = (parents[:, :, None] == slot_ids[None, None, :]).astype(jnp.float32)
    reachable = parent_links + jnp.eye(draft_tree, dtype=jnp.float32)[None]
    for squaring in range(max(1, (draft_tree - 1).bit_length())):
        product = jnp.einsum("rij,rjk->rik", reachable, reachable, precision=lax.Precision.HIGHEST)
        reachable = (product > 0.5).astype(jnp.float32)
    return reachable > 0.5


def row_reduce(partial, axis_name, sent=jnp.float32):
    count = lax.axis_size(axis_name)
    rows, cols = partial.shape
    pieces = partial.reshape(rows, count, cols // count).transpose(1, 0, 2).astype(sent)
    received = lax.all_to_all(pieces, axis_name, 0, 0)
    return jnp.sum(received.astype(jnp.float32), axis=0)


def row_gather(value, axis_name):
    count = lax.axis_size(axis_name)
    copies = jnp.broadcast_to(value[None], (count,) + value.shape)
    return lax.all_to_all(copies, axis_name, 0, 0)


def shards(hidden_in, norm_gain, w_qkv, w_out, cache_k, value_cache, cache_len, parents):
    rows_here = hidden_in.shape[0]
    request_list = cache_k.shape[0]
    token_positions = cache_k.shape[1]
    draft_tree = parents.shape[1]
    head_groups = QUERY_HEADS // KEY_VALUE_HEADS
    row_count = lax.axis_size("row")
    heads_dev = QUERY_HEADS // row_count
    row_index = lax.axis_index("row")
    score_scale = HEAD_SIZE ** (-0.5)
    features = hidden_in.astype(jnp.float32)
    squares = jnp.sum(row_gather(jnp.sum(features * features, axis=1), "row"), axis=0)
    row_scale = lax.rsqrt(squares / D + 1e-05)
    normed = (features * row_scale[:, None] * norm_gain.astype(jnp.float32)[None, :]).astype(
        jnp.bfloat16
    )
    qkv_width = w_qkv.shape[1]
    col_count = lax.axis_size("col")
    weights_all = lax.all_gather(jnp.concatenate([w_qkv, w_out], axis=1), "col", axis=1, tiled=False)
    qkv_all = weights_all[:, :, :qkv_width].reshape(w_qkv.shape[0], col_count * qkv_width)
    out_all = weights_all[:, :, qkv_width:].reshape(w_out.shape[0], -1)
    partial_value = jnp.dot(normed, qkv_all, preferred_element_type=jnp.float32)
    local = jnp.stack([cache_k[0], value_cache[0]]).reshape(
        2, token_positions, KEY_VALUE_HEADS, HEAD_SIZE
    ).transpose(2, 0, 1, 3)
    pieces = jnp.repeat(local, row_count // KEY_VALUE_HEADS, axis=0)
    by_head = lax.all_to_all(pieces, "row", 0, 0)
    by_head, partial_value = lax.optimization_barrier((by_head, partial_value))
    keys = by_head[:, 0].reshape(row_count * token_positions, HEAD_SIZE)
    values = by_head[:, 1].reshape(row_count * token_positions, HEAD_SIZE)
    query_cols = QUERY_HEADS * HEAD_SIZE
    query_part = partial_value[:, :query_cols].reshape(rows_here, row_count, -1)
    pair_part = (
        partial_value[:, query_cols:]
        .reshape(rows_here, 2, KEY_VALUE_HEADS, HEAD_SIZE)
        .transpose(0, 2, 1, 3)
        .reshape(rows_here, row_count, -1)
    )
    owned = jnp.concatenate([query_part, pair_part], axis=2).transpose(1, 0, 2)
    summed = jnp.sum(lax.all_to_all(owned, "row", 0, 0), axis=0).astype(jnp.bfloat16)
    query_mine = summed[:, : heads_dev * HEAD_SIZE]
    pair_mine = summed[:, heads_dev * HEAD_SIZE :]
    partner = [(i, i ^ 1) for i in range(row_count)]
    pair_theirs = lax.ppermute(pair_mine, "row", partner)
    is_key = row_index % 2 == 0
    key_mine = jnp.where(is_key, pair_mine, pair_theirs)
    value_mine = jnp.where(is_key, pair_theirs, pair_mine)
    window = row_count * token_positions
    query_own = query_mine.reshape(draft_tree, heads_dev, HEAD_SIZE)
    scores = (
        jnp.einsum("thd,pd->htp", query_own, keys, preferred_element_type=jnp.float32)
        * score_scale
    )
    visible = (jnp.arange(window, dtype=jnp.int32) < cache_len[0])[None, None, :]
    scores = jnp.where(visible, scores, masked_score)
    allowed = ancestors(parents)[0][None, :, :]
    tree_scores = (
        jnp.einsum("thd,sd->hts", query_own, key_mine, preferred_element_type=jnp.float32)
        * score_scale
    )
    tree_scores = jnp.where(allowed, tree_scores, masked_score)
    highest = jnp.maximum(jnp.max(scores, axis=-1), jnp.max(tree_scores, axis=-1))
    weights = jnp.where(visible, jnp.exp(scores - highest[..., None]), 0.0)
    tree_weights = jnp.where(allowed, jnp.exp(tree_scores - highest[..., None]), 0.0)
    totals = jnp.sum(weights, axis=-1) + jnp.sum(tree_weights, axis=-1)
    blended = jnp.einsum(
        "htp,pd->htd", weights.astype(jnp.bfloat16), values, preferred_element_type=jnp.float32
    ) + jnp.einsum(
        "hts,sd->htd", tree_weights.astype(jnp.bfloat16), value_mine, preferred_element_type=jnp.float32
    )
    attended = (blended / totals[..., None]).astype(jnp.bfloat16)
    attended = attended.transpose(1, 0, 2).reshape(rows_here, heads_dev * HEAD_SIZE)
    partial_out = jnp.dot(
        attended,
        out_all,
        preferred_element_type=jnp.float32,
    )
    return row_reduce(partial_out, "row", jnp.bfloat16).astype(jnp.bfloat16)


def solution(mesh):
    placed = (
        P("col", "row"),
        P("row"),
        P("row", "col"),
        P("row", "col"),
        P("col", "row", None),
        P("col", "row", None),
        P("col"),
        P("col", None),
    )
    return jax.shard_map(
        shards, mesh=mesh, in_specs=placed, out_specs=P("col", "row"), check_vma=False
    )
```

```python
import jax
import jax.numpy as jnp
from jax import lax
from jax.sharding import PartitionSpec as P

D = 4096
QUERY_HEADS = 32
KEY_VALUE_HEADS = 8
HEAD_SIZE = 128


masked_score = -1e30


def ancestors(parents):
    draft_tree = parents.shape[1]
    slot_ids = jnp.arange(draft_tree, dtype=jnp.int32)
    parent_links = (parents[:, :, None] == slot_ids[None, None, :]).astype(jnp.float32)
    reachable = parent_links + jnp.eye(draft_tree, dtype=jnp.float32)[None]
    for squaring in range(max(1, (draft_tree - 1).bit_length())):
        product = jnp.einsum("rij,rjk->rik", reachable, reachable, precision=lax.Precision.HIGHEST)
        reachable = (product > 0.5).astype(jnp.float32)
    return reachable > 0.5


def row_reduce(partial, axis_name, sent=jnp.float32):
    count = lax.axis_size(axis_name)
    rows, cols = partial.shape
    pieces = partial.reshape(rows, count, cols // count).transpose(1, 0, 2).astype(sent)
    received = lax.all_to_all(pieces, axis_name, 0, 0)
    return jnp.sum(received.astype(jnp.float32), axis=0)


def row_gather(value, axis_name):
    count = lax.axis_size(axis_name)
    copies = jnp.broadcast_to(value[None], (count,) + value.shape)
    return lax.all_to_all(copies, axis_name, 0, 0)


def shards(hidden_in, norm_gain, w_qkv, w_out, cache_k, value_cache, cache_len, parents):
    rows_here = hidden_in.shape[0]
    request_list = cache_k.shape[0]
    token_positions = cache_k.shape[1]
    draft_tree = parents.shape[1]
    head_groups = QUERY_HEADS // KEY_VALUE_HEADS
    row_count = lax.axis_size("row")
    heads_dev = QUERY_HEADS // row_count
    row_index = lax.axis_index("row")
    score_scale = HEAD_SIZE ** (-0.5)
    features = hidden_in.astype(jnp.float32)
    squares = jnp.sum(row_gather(jnp.sum(features * features, axis=1), "row"), axis=0)
    row_scale = lax.rsqrt(squares / D + 1e-05)
    normed = (features * row_scale[:, None] * norm_gain.astype(jnp.float32)[None, :]).astype(
        jnp.bfloat16
    )
    qkv_width = w_qkv.shape[1]
    col_count = lax.axis_size("col")
    weights_all = lax.all_gather(jnp.concatenate([w_qkv, w_out], axis=1), "col", axis=1, tiled=True)
    weights_all = lax.optimization_barrier(weights_all)
    partial_all = jnp.dot(
        normed, weights_all, preferred_element_type=jnp.float32
    ).reshape(rows_here, col_count, -1)
    partial_value = partial_all[:, :, :qkv_width].reshape(rows_here, col_count * qkv_width)

    local = jnp.stack([cache_k[0], value_cache[0]]).reshape(
        2, token_positions, KEY_VALUE_HEADS, HEAD_SIZE
    ).transpose(2, 0, 1, 3)
    pieces = jnp.repeat(local, row_count // KEY_VALUE_HEADS, axis=0)
    by_head = lax.all_to_all(pieces, "row", 0, 0)
    by_head, partial_value = lax.optimization_barrier((by_head, partial_value))
    keys = by_head[:, 0].reshape(row_count * token_positions, HEAD_SIZE)
    values = by_head[:, 1].reshape(row_count * token_positions, HEAD_SIZE)
    query_cols = QUERY_HEADS * HEAD_SIZE
    query_part = partial_value[:, :query_cols].reshape(rows_here, row_count, -1)
    pair_part = (
        partial_value[:, query_cols:]
        .reshape(rows_here, 2, KEY_VALUE_HEADS, HEAD_SIZE)
        .transpose(0, 2, 1, 3)
        .reshape(rows_here, row_count, -1)
    )
    owned = jnp.concatenate([query_part, pair_part], axis=2).transpose(1, 0, 2)
    summed = jnp.sum(lax.all_to_all(owned, "row", 0, 0), axis=0).astype(jnp.bfloat16)
    query_mine = summed[:, : heads_dev * HEAD_SIZE]
    pair_mine = summed[:, heads_dev * HEAD_SIZE :]
    partner = [(i, i ^ 1) for i in range(row_count)]
    pair_theirs = lax.ppermute(pair_mine, "row", partner)
    is_key = row_index % 2 == 0
    key_mine = jnp.where(is_key, pair_mine, pair_theirs)
    value_mine = jnp.where(is_key, pair_theirs, pair_mine)
    window = row_count * token_positions
    query_own = query_mine.reshape(draft_tree, heads_dev, HEAD_SIZE)
    scores = (
        jnp.einsum("thd,pd->htp", query_own, keys, preferred_element_type=jnp.float32)
        * score_scale
    )
    visible = (jnp.arange(window, dtype=jnp.int32) < cache_len[0])[None, None, :]
    scores = jnp.where(visible, scores, masked_score)
    allowed = ancestors(parents)[0][None, :, :]
    tree_scores = (
        jnp.einsum("thd,sd->hts", query_own, key_mine, preferred_element_type=jnp.float32)
        * score_scale
    )
    tree_scores = jnp.where(allowed, tree_scores, masked_score)
    highest = jnp.maximum(jnp.max(scores, axis=-1), jnp.max(tree_scores, axis=-1))
    weights = jnp.where(visible, jnp.exp(scores - highest[..., None]), 0.0)
    tree_weights = jnp.where(allowed, jnp.exp(tree_scores - highest[..., None]), 0.0)
    totals = jnp.sum(weights, axis=-1) + jnp.sum(tree_weights, axis=-1)
    blended = jnp.einsum(
        "htp,pd->htd", weights.astype(jnp.bfloat16), values, preferred_element_type=jnp.float32
    ) + jnp.einsum(
        "hts,sd->htd", tree_weights.astype(jnp.bfloat16), value_mine, preferred_element_type=jnp.float32
    )
    attended = (blended / totals[..., None]).astype(jnp.bfloat16)
    attended = attended.transpose(1, 0, 2).reshape(rows_here, heads_dev * HEAD_SIZE)
    partial_out = jnp.dot(
        attended, weights_all, preferred_element_type=jnp.float32
    ).reshape(rows_here, col_count, -1)[:, :, qkv_width:].reshape(rows_here, -1)
    return row_reduce(partial_out, "row", jnp.bfloat16).astype(jnp.bfloat16)


def solution(mesh):
    placed = (
        P("col", "row"),
        P("row"),
        P("row", "col"),
        P("row", "col"),
        P("col", "row", None),
        P("col", "row", None),
        P("col"),
        P("col", None),
    )
    return jax.shard_map(
        shards, mesh=mesh, in_specs=placed, out_specs=P("col", "row"), check_vma=False
    )
```

```python
import jax
import jax.numpy as jnp
from jax import lax
from jax.sharding import PartitionSpec as P

D = 4096
QUERY_HEADS = 32
KEY_VALUE_HEADS = 8
HEAD_SIZE = 128


masked_score = -1e30


def ancestors(parents):
    draft_tree = parents.shape[1]
    slot_ids = jnp.arange(draft_tree, dtype=jnp.int32)
    parent_links = (parents[:, :, None] == slot_ids[None, None, :]).astype(jnp.float32)
    reachable = parent_links + jnp.eye(draft_tree, dtype=jnp.float32)[None]
    for squaring in range(max(1, (draft_tree - 1).bit_length())):
        product = jnp.einsum("rij,rjk->rik", reachable, reachable, precision=lax.Precision.HIGHEST)
        reachable = (product > 0.5).astype(jnp.float32)
    return reachable > 0.5


def row_reduce(partial, axis_name, sent=jnp.float32):
    count = lax.axis_size(axis_name)
    rows, cols = partial.shape
    pieces = partial.reshape(rows, count, cols // count).transpose(1, 0, 2).astype(sent)
    received = lax.all_to_all(pieces, axis_name, 0, 0)
    return jnp.sum(received.astype(jnp.float32), axis=0)


def row_gather(value, axis_name):
    count = lax.axis_size(axis_name)
    copies = jnp.broadcast_to(value[None], (count,) + value.shape)
    return lax.all_to_all(copies, axis_name, 0, 0)


def shards(hidden_in, norm_gain, w_qkv, w_out, cache_k, value_cache, cache_len, parents):
    rows_here = hidden_in.shape[0]
    request_list = cache_k.shape[0]
    token_positions = cache_k.shape[1]
    draft_tree = parents.shape[1]
    head_groups = QUERY_HEADS // KEY_VALUE_HEADS
    row_count = lax.axis_size("row")
    heads_dev = QUERY_HEADS // row_count
    row_index = lax.axis_index("row")
    score_scale = HEAD_SIZE ** (-0.5)
    features = hidden_in.astype(jnp.float32)
    squares = jnp.sum(row_gather(jnp.sum(features * features, axis=1), "row"), axis=0)
    row_scale = lax.rsqrt(squares / D + 1e-05)
    normed = (features * row_scale[:, None] * norm_gain.astype(jnp.float32)[None, :]).astype(
        jnp.bfloat16
    )
    qkv_width = w_qkv.shape[1]
    col_count = lax.axis_size("col")
    weights_all = lax.all_gather(jnp.concatenate([w_qkv, w_out], axis=1), "col", axis=1, tiled=True)
    weights_all = lax.optimization_barrier(weights_all)
    partial_all = jnp.dot(
        normed, weights_all, preferred_element_type=jnp.float32
    ).reshape(rows_here, col_count, -1)
    partial_value = partial_all[:, :, :qkv_width].reshape(rows_here, col_count * qkv_width)

    local = jnp.stack([cache_k[0], value_cache[0]]).reshape(
        2, token_positions, KEY_VALUE_HEADS, HEAD_SIZE
    ).transpose(2, 0, 1, 3)
    pieces = jnp.repeat(local, row_count // KEY_VALUE_HEADS, axis=0)
    by_head = lax.all_to_all(pieces, "row", 0, 0)
    by_head, partial_value = lax.optimization_barrier((by_head, partial_value))
    keys = by_head[:, 0].reshape(row_count * token_positions, HEAD_SIZE)
    values = by_head[:, 1].reshape(row_count * token_positions, HEAD_SIZE)
    query_cols = QUERY_HEADS * HEAD_SIZE
    query_part = partial_value[:, :query_cols].reshape(rows_here, row_count, -1)
    pair_part = (
        partial_value[:, query_cols:]
        .reshape(rows_here, 2, KEY_VALUE_HEADS, HEAD_SIZE)
        .transpose(0, 2, 1, 3)
        .reshape(rows_here, row_count, -1)
    )
    owned = jnp.concatenate([query_part, pair_part], axis=2).transpose(1, 0, 2)
    summed = jnp.sum(lax.all_to_all(owned, "row", 0, 0), axis=0).astype(jnp.bfloat16)
    query_mine = summed[:, : heads_dev * HEAD_SIZE]
    pair_mine = summed[:, heads_dev * HEAD_SIZE :]
    partner = [(i, i ^ 1) for i in range(row_count)]
    pair_theirs = lax.ppermute(pair_mine, "row", partner)
    is_key = row_index % 2 == 0
    key_mine = jnp.where(is_key, pair_mine, pair_theirs)
    value_mine = jnp.where(is_key, pair_theirs, pair_mine)
    window = row_count * token_positions
    query_own = query_mine.reshape(draft_tree, heads_dev, HEAD_SIZE)
    scores = (
        jnp.einsum("thd,pd->htp", query_own, keys, preferred_element_type=jnp.float32)
        * score_scale
    )
    visible = (jnp.arange(window, dtype=jnp.int32) < cache_len[0])[None, None, :]
    scores = jnp.where(visible, scores, masked_score)
    allowed = ancestors(parents)[0][None, :, :]
    tree_scores = (
        jnp.einsum("thd,sd->hts", query_own, key_mine, preferred_element_type=jnp.float32)
        * score_scale
    )
    tree_scores = jnp.where(allowed, tree_scores, masked_score)
    highest = jnp.maximum(jnp.max(scores, axis=-1), jnp.max(tree_scores, axis=-1))
    weights = jnp.where(visible, jnp.exp(scores - highest[..., None]), 0.0)
    tree_weights = jnp.where(allowed, jnp.exp(tree_scores - highest[..., None]), 0.0)
    totals = jnp.sum(weights, axis=-1) + jnp.sum(tree_weights, axis=-1)
    blended = jnp.einsum(
        "htp,pd->htd", weights.astype(jnp.bfloat16), values, preferred_element_type=jnp.float32
    ) + jnp.einsum(
        "hts,sd->htd", tree_weights.astype(jnp.bfloat16), value_mine, preferred_element_type=jnp.float32
    )
    attended = (blended / totals[..., None]).astype(jnp.bfloat16)
    attended = attended.transpose(1, 0, 2).reshape(rows_here, heads_dev * HEAD_SIZE)
    out_all = weights_all.reshape(w_out.shape[0], col_count, -1)[:, :, qkv_width:]
    partial_out = jnp.dot(
        attended, out_all.reshape(w_out.shape[0], -1), preferred_element_type=jnp.float32
    )
    return row_reduce(partial_out, "row", jnp.bfloat16).astype(jnp.bfloat16)


def solution(mesh):
    placed = (
        P("col", "row"),
        P("row"),
        P("row", "col"),
        P("row", "col"),
        P("col", "row", None),
        P("col", "row", None),
        P("col"),
        P("col", None),
    )
    return jax.shard_map(
        shards, mesh=mesh, in_specs=placed, out_specs=P("col", "row"), check_vma=False
    )
```

```python
import jax
import jax.numpy as jnp
from jax import lax
from jax.sharding import PartitionSpec as P

D = 4096
QUERY_HEADS = 32
KEY_VALUE_HEADS = 8
HEAD_SIZE = 128


masked_score = -1e30


def ancestors(parents):
    draft_tree = parents.shape[1]
    slot_ids = jnp.arange(draft_tree, dtype=jnp.int32)
    parent_links = (parents[:, :, None] == slot_ids[None, None, :]).astype(jnp.float32)
    reachable = parent_links + jnp.eye(draft_tree, dtype=jnp.float32)[None]
    for squaring in range(max(1, (draft_tree - 1).bit_length())):
        product = jnp.einsum("rij,rjk->rik", reachable, reachable, precision=lax.Precision.HIGHEST)
        reachable = (product > 0.5).astype(jnp.float32)
    return reachable > 0.5


def row_reduce(partial, axis_name, sent=jnp.float32):
    count = lax.axis_size(axis_name)
    rows, cols = partial.shape
    pieces = partial.reshape(rows, count, cols // count).transpose(1, 0, 2).astype(sent)
    received = lax.all_to_all(pieces, axis_name, 0, 0)
    return jnp.sum(received.astype(jnp.float32), axis=0)


def row_gather(value, axis_name):
    count = lax.axis_size(axis_name)
    copies = jnp.broadcast_to(value[None], (count,) + value.shape)
    return lax.all_to_all(copies, axis_name, 0, 0)


def shards(hidden_in, norm_gain, w_qkv, w_out, cache_k, value_cache, cache_len, parents):
    rows_here = hidden_in.shape[0]
    request_list = cache_k.shape[0]
    token_positions = cache_k.shape[1]
    draft_tree = parents.shape[1]
    head_groups = QUERY_HEADS // KEY_VALUE_HEADS
    row_count = lax.axis_size("row")
    heads_dev = QUERY_HEADS // row_count
    row_index = lax.axis_index("row")
    score_scale = HEAD_SIZE ** (-0.5)
    features = hidden_in.astype(jnp.float32)
    squares = jnp.sum(row_gather(jnp.sum(features * features, axis=1), "row"), axis=0)
    row_scale = lax.rsqrt(squares / D + 1e-05)
    normed = (features * row_scale[:, None] * norm_gain.astype(jnp.float32)[None, :]).astype(
        jnp.bfloat16
    )
    qkv_width = w_qkv.shape[1]
    col_count = lax.axis_size("col")
    weights_all = lax.all_gather(jnp.concatenate([w_qkv, w_out], axis=1), "col", axis=1, tiled=True)
    weights_all = lax.optimization_barrier(weights_all)
    partial_all = jnp.dot(
        normed, weights_all, preferred_element_type=jnp.float32
    ).reshape(rows_here, col_count, -1)
    partial_value = partial_all[:, :, :qkv_width].reshape(rows_here, col_count * qkv_width)

    local = jnp.stack([cache_k[0], value_cache[0]]).reshape(
        2, token_positions, KEY_VALUE_HEADS, HEAD_SIZE
    ).transpose(2, 0, 1, 3)
    pieces = jnp.repeat(local, row_count // KEY_VALUE_HEADS, axis=0)
    by_head = lax.all_to_all(pieces, "row", 0, 0)
    by_head, partial_value = lax.optimization_barrier((by_head, partial_value))
    keys = by_head[:, 0].reshape(row_count * token_positions, HEAD_SIZE)
    values = by_head[:, 1].reshape(row_count * token_positions, HEAD_SIZE)
    query_cols = QUERY_HEADS * HEAD_SIZE
    query_part = partial_value[:, :query_cols].reshape(rows_here, row_count, -1)
    pair_part = (
        partial_value[:, query_cols:]
        .reshape(rows_here, 2, KEY_VALUE_HEADS, HEAD_SIZE)
        .transpose(0, 2, 1, 3)
        .reshape(rows_here, row_count, -1)
    )
    owned = jnp.concatenate([query_part, pair_part], axis=2).transpose(1, 0, 2)
    side = 4
    along_x = [[y * side + x for x in range(side)] for y in range(side)]
    along_y = [[y * side + x for y in range(side)] for x in range(side)]
    owned = owned.reshape(side, side, rows_here, -1)
    first = lax.all_to_all(owned, "row", 1, 1, axis_index_groups=along_x)
    first = jnp.sum(first, axis=1)
    second = lax.all_to_all(first, "row", 0, 0, axis_index_groups=along_y)
    summed = jnp.sum(second, axis=0).astype(jnp.bfloat16)
    query_mine = summed[:, : heads_dev * HEAD_SIZE]
    pair_mine = summed[:, heads_dev * HEAD_SIZE :]
    partner = [(i, i ^ 1) for i in range(row_count)]
    pair_theirs = lax.ppermute(pair_mine, "row", partner)
    is_key = row_index % 2 == 0
    key_mine = jnp.where(is_key, pair_mine, pair_theirs)
    value_mine = jnp.where(is_key, pair_theirs, pair_mine)
    window = row_count * token_positions
    query_own = query_mine.reshape(draft_tree, heads_dev, HEAD_SIZE)
    scores = (
        jnp.einsum("thd,pd->htp", query_own, keys, preferred_element_type=jnp.float32)
        * score_scale
    )
    visible = (jnp.arange(window, dtype=jnp.int32) < cache_len[0])[None, None, :]
    scores = jnp.where(visible, scores, masked_score)
    allowed = ancestors(parents)[0][None, :, :]
    tree_scores = (
        jnp.einsum("thd,sd->hts", query_own, key_mine, preferred_element_type=jnp.float32)
        * score_scale
    )
    tree_scores = jnp.where(allowed, tree_scores, masked_score)
    highest = jnp.maximum(jnp.max(scores, axis=-1), jnp.max(tree_scores, axis=-1))
    weights = jnp.where(visible, jnp.exp(scores - highest[..., None]), 0.0)
    tree_weights = jnp.where(allowed, jnp.exp(tree_scores - highest[..., None]), 0.0)
    totals = jnp.sum(weights, axis=-1) + jnp.sum(tree_weights, axis=-1)
    blended = jnp.einsum(
        "htp,pd->htd", weights.astype(jnp.bfloat16), values, preferred_element_type=jnp.float32
    ) + jnp.einsum(
        "hts,sd->htd", tree_weights.astype(jnp.bfloat16), value_mine, preferred_element_type=jnp.float32
    )
    attended = (blended / totals[..., None]).astype(jnp.bfloat16)
    attended = attended.transpose(1, 0, 2).reshape(rows_here, heads_dev * HEAD_SIZE)
    out_all = weights_all.reshape(w_out.shape[0], col_count, -1)[:, :, qkv_width:]
    partial_out = jnp.dot(
        attended, out_all.reshape(w_out.shape[0], -1), preferred_element_type=jnp.float32
    )
    return row_reduce(partial_out, "row", jnp.bfloat16).astype(jnp.bfloat16)


def solution(mesh):
    placed = (
        P("col", "row"),
        P("row"),
        P("row", "col"),
        P("row", "col"),
        P("col", "row", None),
        P("col", "row", None),
        P("col"),
        P("col", None),
    )
    return jax.shard_map(
        shards, mesh=mesh, in_specs=placed, out_specs=P("col", "row"), check_vma=False
    )
```

```python
import jax
import jax.numpy as jnp
from jax import lax
from jax.sharding import PartitionSpec as P

D = 4096
QUERY_HEADS = 32
KEY_VALUE_HEADS = 8
HEAD_SIZE = 128


masked_score = -1e30


def ancestors(parents):
    draft_tree = parents.shape[1]
    slot_ids = jnp.arange(draft_tree, dtype=jnp.int32)
    parent_links = (parents[:, :, None] == slot_ids[None, None, :]).astype(jnp.float32)
    reachable = parent_links + jnp.eye(draft_tree, dtype=jnp.float32)[None]
    for squaring in range(max(1, (draft_tree - 1).bit_length())):
        product = jnp.einsum("rij,rjk->rik", reachable, reachable, precision=lax.Precision.HIGHEST)
        reachable = (product > 0.5).astype(jnp.float32)
    return reachable > 0.5


def row_reduce(partial, axis_name, sent=jnp.float32):
    count = lax.axis_size(axis_name)
    rows, cols = partial.shape
    pieces = partial.reshape(rows, count, cols // count).transpose(1, 0, 2).astype(sent)
    received = lax.all_to_all(pieces, axis_name, 0, 0)
    return jnp.sum(received.astype(jnp.float32), axis=0)


def row_gather(value, axis_name):
    count = lax.axis_size(axis_name)
    copies = jnp.broadcast_to(value[None], (count,) + value.shape)
    return lax.all_to_all(copies, axis_name, 0, 0)


def shards(hidden_in, norm_gain, w_qkv, w_out, cache_k, value_cache, cache_len, parents):
    rows_here = hidden_in.shape[0]
    request_list = cache_k.shape[0]
    token_positions = cache_k.shape[1]
    draft_tree = parents.shape[1]
    head_groups = QUERY_HEADS // KEY_VALUE_HEADS
    row_count = lax.axis_size("row")
    heads_dev = QUERY_HEADS // row_count
    row_index = lax.axis_index("row")
    score_scale = HEAD_SIZE ** (-0.5)
    features = hidden_in.astype(jnp.float32)
    squares = jnp.sum(row_gather(jnp.sum(features * features, axis=1), "row"), axis=0)
    row_scale = lax.rsqrt(squares / D + 1e-05)
    normed = (features * row_scale[:, None] * norm_gain.astype(jnp.float32)[None, :]).astype(
        jnp.bfloat16
    )
    qkv_width = w_qkv.shape[1]
    col_count = lax.axis_size("col")
    weights_all = lax.all_gather(jnp.concatenate([w_qkv, w_out], axis=1), "col", axis=1, tiled=True)
    weights_all = lax.optimization_barrier(weights_all)
    partial_all = jnp.dot(
        normed, weights_all, preferred_element_type=jnp.float32
    ).reshape(rows_here, col_count, -1)
    partial_value = partial_all[:, :, :qkv_width].reshape(rows_here, col_count * qkv_width)

    local = jnp.stack([cache_k[0], value_cache[0]]).reshape(
        2, token_positions, KEY_VALUE_HEADS, HEAD_SIZE
    ).transpose(2, 0, 1, 3)
    pieces = jnp.repeat(local, row_count // KEY_VALUE_HEADS, axis=0)
    by_head = lax.all_to_all(pieces, "row", 0, 0)
    by_head, partial_value = lax.optimization_barrier((by_head, partial_value))
    keys = by_head[:, 0].reshape(row_count * token_positions, HEAD_SIZE)
    values = by_head[:, 1].reshape(row_count * token_positions, HEAD_SIZE)
    query_cols = QUERY_HEADS * HEAD_SIZE
    query_part = partial_value[:, :query_cols].reshape(rows_here, row_count, -1)
    pair_part = (
        partial_value[:, query_cols:]
        .reshape(rows_here, 2, KEY_VALUE_HEADS, HEAD_SIZE)
        .transpose(0, 2, 1, 3)
        .reshape(rows_here, row_count, -1)
    )
    owned = jnp.concatenate([query_part, pair_part], axis=2).transpose(1, 0, 2)
    summed = jnp.sum(lax.all_to_all(owned, "row", 0, 0), axis=0).astype(jnp.bfloat16)
    query_mine = summed[:, : heads_dev * HEAD_SIZE]
    pair_mine = summed[:, heads_dev * HEAD_SIZE :]
    partner = [(i, i ^ 1) for i in range(row_count)]
    pair_theirs = lax.ppermute(pair_mine, "row", partner)
    is_key = row_index % 2 == 0
    key_mine = jnp.where(is_key, pair_mine, pair_theirs)
    value_mine = jnp.where(is_key, pair_theirs, pair_mine)
    window = row_count * token_positions
    query_own = query_mine.reshape(draft_tree, heads_dev, HEAD_SIZE)
    scores = (
        jnp.einsum("thd,pd->htp", query_own, keys, preferred_element_type=jnp.float32)
        * score_scale
    )
    visible = (jnp.arange(window, dtype=jnp.int32) < cache_len[0])[None, None, :]
    scores = jnp.where(visible, scores, masked_score)
    allowed = ancestors(parents)[0][None, :, :]
    tree_scores = (
        jnp.einsum("thd,sd->hts", query_own, key_mine, preferred_element_type=jnp.float32)
        * score_scale
    )
    tree_scores = jnp.where(allowed, tree_scores, masked_score)
    cache_max = jnp.max(scores, axis=-1)
    weights = jnp.where(visible, jnp.exp(scores - cache_max[..., None]), 0.0)
    cache_total = jnp.sum(weights, axis=-1)
    cache_blend = jnp.einsum(
        "htp,pd->htd", weights.astype(jnp.bfloat16), values, preferred_element_type=jnp.float32
    )
    cache_max, cache_total, cache_blend, tree_scores, value_mine = lax.optimization_barrier(
        (cache_max, cache_total, cache_blend, tree_scores, value_mine)
    )
    tree_max = jnp.max(tree_scores, axis=-1)
    tree_weights = jnp.where(allowed, jnp.exp(tree_scores - tree_max[..., None]), 0.0)
    tree_total = jnp.sum(tree_weights, axis=-1)
    tree_blend = jnp.einsum(
        "hts,sd->htd", tree_weights.astype(jnp.bfloat16), value_mine, preferred_element_type=jnp.float32
    )
    joint_max = jnp.maximum(cache_max, tree_max)
    cache_scale = jnp.exp(cache_max - joint_max)
    tree_scale = jnp.exp(tree_max - joint_max)
    totals = cache_total * cache_scale + tree_total * tree_scale
    blended = cache_blend * cache_scale[..., None] + tree_blend * tree_scale[..., None]
    attended = (blended / totals[..., None]).astype(jnp.bfloat16)
    attended = attended.transpose(1, 0, 2).reshape(rows_here, heads_dev * HEAD_SIZE)
    out_all = weights_all.reshape(w_out.shape[0], col_count, -1)[:, :, qkv_width:]
    partial_out = jnp.dot(
        attended, out_all.reshape(w_out.shape[0], -1), preferred_element_type=jnp.float32
    )
    return row_reduce(partial_out, "row", jnp.bfloat16).astype(jnp.bfloat16)


def solution(mesh):
    placed = (
        P("col", "row"),
        P("row"),
        P("row", "col"),
        P("row", "col"),
        P("col", "row", None),
        P("col", "row", None),
        P("col"),
        P("col", None),
    )
    return jax.shard_map(
        shards, mesh=mesh, in_specs=placed, out_specs=P("col", "row"), check_vma=False
    )
```

```python
import jax
import jax.numpy as jnp
from jax import lax
from jax.sharding import PartitionSpec as P

D = 4096
QUERY_HEADS = 32
KEY_VALUE_HEADS = 8
HEAD_SIZE = 128


masked_score = -1e30


def ancestors(parents):
    draft_tree = parents.shape[1]
    slot_ids = jnp.arange(draft_tree, dtype=jnp.int32)
    parent_links = (parents[:, :, None] == slot_ids[None, None, :]).astype(jnp.float32)
    reachable = parent_links + jnp.eye(draft_tree, dtype=jnp.float32)[None]
    for squaring in range(max(1, (draft_tree - 1).bit_length())):
        product = jnp.einsum("rij,rjk->rik", reachable, reachable, precision=lax.Precision.HIGHEST)
        reachable = (product > 0.5).astype(jnp.float32)
    return reachable > 0.5


def row_reduce(partial, axis_name, sent=jnp.float32):
    count = lax.axis_size(axis_name)
    rows, cols = partial.shape
    pieces = partial.reshape(rows, count, cols // count).transpose(1, 0, 2).astype(sent)
    received = lax.all_to_all(pieces, axis_name, 0, 0)
    return jnp.sum(received.astype(jnp.float32), axis=0)


def row_gather(value, axis_name):
    count = lax.axis_size(axis_name)
    copies = jnp.broadcast_to(value[None], (count,) + value.shape)
    return lax.all_to_all(copies, axis_name, 0, 0)


def shards(hidden_in, norm_gain, w_qkv, w_out, cache_k, value_cache, cache_len, parents):
    rows_here = hidden_in.shape[0]
    request_list = cache_k.shape[0]
    token_positions = cache_k.shape[1]
    draft_tree = parents.shape[1]
    head_groups = QUERY_HEADS // KEY_VALUE_HEADS
    row_count = lax.axis_size("row")
    heads_dev = QUERY_HEADS // row_count
    row_index = lax.axis_index("row")
    score_scale = HEAD_SIZE ** (-0.5)
    features = hidden_in.astype(jnp.float32)
    squares = jnp.sum(row_gather(jnp.sum(features * features, axis=1), "row"), axis=0)
    row_scale = lax.rsqrt(squares / D + 1e-05)
    normed = (features * row_scale[:, None] * norm_gain.astype(jnp.float32)[None, :]).astype(
        jnp.bfloat16
    )
    qkv_width = w_qkv.shape[1]
    col_count = lax.axis_size("col")
    out_padded = jnp.pad(w_out, ((0, 0), (0, qkv_width - w_out.shape[1])))
    weights_all = lax.all_gather(jnp.stack([w_qkv, out_padded]), "col", axis=2, tiled=True)
    weights_all = lax.optimization_barrier(weights_all)
    partial_value = jnp.dot(normed, weights_all[0], preferred_element_type=jnp.float32)

    local = jnp.stack([cache_k[0], value_cache[0]]).reshape(
        2, token_positions, KEY_VALUE_HEADS, HEAD_SIZE
    ).transpose(2, 0, 1, 3)
    pieces = jnp.repeat(local, row_count // KEY_VALUE_HEADS, axis=0)
    by_head = lax.all_to_all(pieces, "row", 0, 0)
    by_head, partial_value = lax.optimization_barrier((by_head, partial_value))
    keys = by_head[:, 0].reshape(row_count * token_positions, HEAD_SIZE)
    values = by_head[:, 1].reshape(row_count * token_positions, HEAD_SIZE)
    query_cols = QUERY_HEADS * HEAD_SIZE
    query_part = partial_value[:, :query_cols].reshape(rows_here, row_count, -1)
    pair_part = (
        partial_value[:, query_cols:]
        .reshape(rows_here, 2, KEY_VALUE_HEADS, HEAD_SIZE)
        .transpose(0, 2, 1, 3)
        .reshape(rows_here, row_count, -1)
    )
    owned = jnp.concatenate([query_part, pair_part], axis=2).transpose(1, 0, 2)
    summed = jnp.sum(lax.all_to_all(owned, "row", 0, 0), axis=0).astype(jnp.bfloat16)
    query_mine = summed[:, : heads_dev * HEAD_SIZE]
    pair_mine = summed[:, heads_dev * HEAD_SIZE :]
    partner = [(i, i ^ 1) for i in range(row_count)]
    pair_theirs = lax.ppermute(pair_mine, "row", partner)
    is_key = row_index % 2 == 0
    key_mine = jnp.where(is_key, pair_mine, pair_theirs)
    value_mine = jnp.where(is_key, pair_theirs, pair_mine)
    window = row_count * token_positions
    query_own = query_mine.reshape(draft_tree, heads_dev, HEAD_SIZE)
    scores = (
        jnp.einsum("thd,pd->htp", query_own, keys, preferred_element_type=jnp.float32)
        * score_scale
    )
    visible = (jnp.arange(window, dtype=jnp.int32) < cache_len[0])[None, None, :]
    scores = jnp.where(visible, scores, masked_score)
    allowed = ancestors(parents)[0][None, :, :]
    tree_scores = (
        jnp.einsum("thd,sd->hts", query_own, key_mine, preferred_element_type=jnp.float32)
        * score_scale
    )
    tree_scores = jnp.where(allowed, tree_scores, masked_score)
    cache_max = jnp.max(scores, axis=-1)
    weights = jnp.where(visible, jnp.exp(scores - cache_max[..., None]), 0.0)
    cache_total = jnp.sum(weights, axis=-1)
    cache_blend = jnp.einsum(
        "htp,pd->htd", weights.astype(jnp.bfloat16), values, preferred_element_type=jnp.float32
    )
    cache_max, cache_total, cache_blend, tree_scores, value_mine = lax.optimization_barrier(
        (cache_max, cache_total, cache_blend, tree_scores, value_mine)
    )
    tree_max = jnp.max(tree_scores, axis=-1)
    tree_weights = jnp.where(allowed, jnp.exp(tree_scores - tree_max[..., None]), 0.0)
    tree_total = jnp.sum(tree_weights, axis=-1)
    tree_blend = jnp.einsum(
        "hts,sd->htd", tree_weights.astype(jnp.bfloat16), value_mine, preferred_element_type=jnp.float32
    )
    joint_max = jnp.maximum(cache_max, tree_max)
    cache_scale = jnp.exp(cache_max - joint_max)
    tree_scale = jnp.exp(tree_max - joint_max)
    totals = cache_total * cache_scale + tree_total * tree_scale
    blended = cache_blend * cache_scale[..., None] + tree_blend * tree_scale[..., None]
    attended = (blended / totals[..., None]).astype(jnp.bfloat16)
    attended = attended.transpose(1, 0, 2).reshape(rows_here, heads_dev * HEAD_SIZE)
    out_all = weights_all[1].reshape(w_out.shape[0], col_count, -1)[:, :, : w_out.shape[1]]
    partial_out = jnp.dot(
        attended, out_all.reshape(w_out.shape[0], -1), preferred_element_type=jnp.float32
    )
    return row_reduce(partial_out, "row", jnp.bfloat16).astype(jnp.bfloat16)


def solution(mesh):
    placed = (
        P("col", "row"),
        P("row"),
        P("row", "col"),
        P("row", "col"),
        P("col", "row", None),
        P("col", "row", None),
        P("col"),
        P("col", None),
    )
    return jax.shard_map(
        shards, mesh=mesh, in_specs=placed, out_specs=P("col", "row"), check_vma=False
    )
```

```python
import jax
import jax.numpy as jnp
from jax import lax
from jax.sharding import PartitionSpec as P

D = 4096
QUERY_HEADS = 32
KEY_VALUE_HEADS = 8
HEAD_SIZE = 128


masked_score = -1e30


def ancestors(parents):
    draft_tree = parents.shape[1]
    slot_ids = jnp.arange(draft_tree, dtype=jnp.int32)
    parent_links = (parents[:, :, None] == slot_ids[None, None, :]).astype(jnp.float32)
    reachable = parent_links + jnp.eye(draft_tree, dtype=jnp.float32)[None]
    for squaring in range(max(1, (draft_tree - 1).bit_length())):
        product = jnp.einsum("rij,rjk->rik", reachable, reachable, precision=lax.Precision.HIGHEST)
        reachable = (product > 0.5).astype(jnp.float32)
    return reachable > 0.5


def row_reduce(partial, axis_name, sent=jnp.float32):
    count = lax.axis_size(axis_name)
    rows, cols = partial.shape
    pieces = partial.reshape(rows, count, cols // count).transpose(1, 0, 2).astype(sent)
    received = lax.all_to_all(pieces, axis_name, 0, 0)
    return jnp.sum(received.astype(jnp.float32), axis=0)


def row_gather(value, axis_name):
    count = lax.axis_size(axis_name)
    copies = jnp.broadcast_to(value[None], (count,) + value.shape)
    return lax.all_to_all(copies, axis_name, 0, 0)


def shards(hidden_in, norm_gain, w_qkv, w_out, cache_k, value_cache, cache_len, parents):
    rows_here = hidden_in.shape[0]
    request_list = cache_k.shape[0]
    token_positions = cache_k.shape[1]
    draft_tree = parents.shape[1]
    head_groups = QUERY_HEADS // KEY_VALUE_HEADS
    row_count = lax.axis_size("row")
    heads_dev = QUERY_HEADS // row_count
    row_index = lax.axis_index("row")
    score_scale = HEAD_SIZE ** (-0.5)
    features = hidden_in.astype(jnp.float32)
    squares = jnp.sum(row_gather(jnp.sum(features * features, axis=1), "row"), axis=0)
    row_scale = lax.rsqrt(squares / D + 1e-05)
    normed = (features * row_scale[:, None] * norm_gain.astype(jnp.float32)[None, :]).astype(
        jnp.bfloat16
    )
    qkv_width = w_qkv.shape[1]
    col_count = lax.axis_size("col")
    feature_rows = w_qkv.shape[0]
    out_rows = -(-w_out.size // qkv_width)
    out_rows = -(-out_rows // 8) * 8
    out_flat = jnp.pad(w_out.reshape(-1), (0, out_rows * qkv_width - w_out.size))
    weights_all = lax.all_gather(
        jnp.concatenate([w_qkv, out_flat.reshape(out_rows, qkv_width)]), "col", axis=1, tiled=True
    )
    weights_all = lax.optimization_barrier(weights_all)
    partial_value = jnp.dot(normed, weights_all[:feature_rows], preferred_element_type=jnp.float32)

    local = jnp.stack([cache_k[0], value_cache[0]]).reshape(
        2, token_positions, KEY_VALUE_HEADS, HEAD_SIZE
    ).transpose(2, 0, 1, 3)
    pieces = jnp.repeat(local, row_count // KEY_VALUE_HEADS, axis=0)
    by_head = lax.all_to_all(pieces, "row", 0, 0)
    by_head, partial_value = lax.optimization_barrier((by_head, partial_value))
    keys = by_head[:, 0].reshape(row_count * token_positions, HEAD_SIZE)
    values = by_head[:, 1].reshape(row_count * token_positions, HEAD_SIZE)
    query_cols = QUERY_HEADS * HEAD_SIZE
    query_part = partial_value[:, :query_cols].reshape(rows_here, row_count, -1)
    pair_part = (
        partial_value[:, query_cols:]
        .reshape(rows_here, 2, KEY_VALUE_HEADS, HEAD_SIZE)
        .transpose(0, 2, 1, 3)
        .reshape(rows_here, row_count, -1)
    )
    owned = jnp.concatenate([query_part, pair_part], axis=2).transpose(1, 0, 2)
    summed = jnp.sum(lax.all_to_all(owned, "row", 0, 0), axis=0).astype(jnp.bfloat16)
    query_mine = summed[:, : heads_dev * HEAD_SIZE]
    pair_mine = summed[:, heads_dev * HEAD_SIZE :]
    partner = [(i, i ^ 1) for i in range(row_count)]
    pair_theirs = lax.ppermute(pair_mine, "row", partner)
    is_key = row_index % 2 == 0
    key_mine = jnp.where(is_key, pair_mine, pair_theirs)
    value_mine = jnp.where(is_key, pair_theirs, pair_mine)
    window = row_count * token_positions
    query_own = query_mine.reshape(draft_tree, heads_dev, HEAD_SIZE)
    scores = (
        jnp.einsum("thd,pd->htp", query_own, keys, preferred_element_type=jnp.float32)
        * score_scale
    )
    visible = (jnp.arange(window, dtype=jnp.int32) < cache_len[0])[None, None, :]
    scores = jnp.where(visible, scores, masked_score)
    allowed = ancestors(parents)[0][None, :, :]
    tree_scores = (
        jnp.einsum("thd,sd->hts", query_own, key_mine, preferred_element_type=jnp.float32)
        * score_scale
    )
    tree_scores = jnp.where(allowed, tree_scores, masked_score)
    cache_max = jnp.max(scores, axis=-1)
    weights = jnp.where(visible, jnp.exp(scores - cache_max[..., None]), 0.0)
    cache_total = jnp.sum(weights, axis=-1)
    cache_blend = jnp.einsum(
        "htp,pd->htd", weights.astype(jnp.bfloat16), values, preferred_element_type=jnp.float32
    )
    cache_max, cache_total, cache_blend, tree_scores, value_mine = lax.optimization_barrier(
        (cache_max, cache_total, cache_blend, tree_scores, value_mine)
    )
    tree_max = jnp.max(tree_scores, axis=-1)
    tree_weights = jnp.where(allowed, jnp.exp(tree_scores - tree_max[..., None]), 0.0)
    tree_total = jnp.sum(tree_weights, axis=-1)
    tree_blend = jnp.einsum(
        "hts,sd->htd", tree_weights.astype(jnp.bfloat16), value_mine, preferred_element_type=jnp.float32
    )
    joint_max = jnp.maximum(cache_max, tree_max)
    cache_scale = jnp.exp(cache_max - joint_max)
    tree_scale = jnp.exp(tree_max - joint_max)
    totals = cache_total * cache_scale + tree_total * tree_scale
    blended = cache_blend * cache_scale[..., None] + tree_blend * tree_scale[..., None]
    attended = (blended / totals[..., None]).astype(jnp.bfloat16)
    attended = attended.transpose(1, 0, 2).reshape(rows_here, heads_dev * HEAD_SIZE)
    out_all = (
        weights_all[feature_rows:]
        .reshape(out_rows, col_count, qkv_width)
        .transpose(1, 0, 2)
        .reshape(col_count, -1)[:, : w_out.size]
        .reshape(col_count, w_out.shape[0], w_out.shape[1])
        .transpose(1, 0, 2)
    )
    partial_out = jnp.dot(
        attended, out_all.reshape(w_out.shape[0], -1), preferred_element_type=jnp.float32
    )
    return row_reduce(partial_out, "row", jnp.bfloat16).astype(jnp.bfloat16)


def solution(mesh):
    placed = (
        P("col", "row"),
        P("row"),
        P("row", "col"),
        P("row", "col"),
        P("col", "row", None),
        P("col", "row", None),
        P("col"),
        P("col", None),
    )
    return jax.shard_map(
        shards, mesh=mesh, in_specs=placed, out_specs=P("col", "row"), check_vma=False
    )
```
